256 devices in a mesh: group: 8 (over z_lo, x), member: 32 (over z_hi, y, core).
Axes of the slice: x: 4, y: 4, z: 8 (z_hi: 4, z_lo: 2; z = z_hi * 2 + z_lo), core: 2. Of those that a mesh axis runs over, the one named last changes fastest.
Arguments:
- entities: bfloat16 [131072, 400], P(('group', 'member')), may hold values from -1.796875 to 1.796875
- hub_rows: bfloat16 [128, 400], replicated, may hold values from -1.796875 to 1.796875
- relations: float32 [2112, 400], replicated
- matching: int32 [8], replicated, may hold values from 0 to 7, as said below
- head_index: int32 [4096, 256], P(('group', 'member')), may hold values from 0 to 511
- tail_index: int32 [4096, 256], P(('group', 'member')), may hold values from 0 to 639
- tile_rel: int32 [4096], P(('group', 'member')), may hold values from 0 to 2111
- tile_count: int32 [8, 32], P('group', 'member'), may hold values from 1 to 16, as said below
Outputs:
- new_entities: bfloat16 [131072, 400], P(('group', 'member'))
- new_hub: bfloat16 [128, 400], replicated
The draws below stay inside these ranges and needn't reach their ends.
Inputs may be any that keep to these rules, and one draw needn't show every extreme that they name: `matching`: a permutation of the partitions. `tile_count`: some device has exactly 16 live tiles.
All inputs are finite; a program needn't handle non-finite values.
Results may differ from the reference program's by a relative error of at most 0.014.
Values may be sent and summed in bfloat16 or wider, within the bound.
No kernel may reach another device: no remote copies, remote signals or barrier semaphores. Data moves between devices by JAX's collectives and lax.ppermute only.
A program may use at most 64 MiB of HBM per device.

```python
import jax
import jax.numpy as jnp
from jax import lax

D = 400
RELS = 2112
HUB = 128
EDGE = 256
ROWS = 512
TILES = 16
GROUPS = 8
MEMBERS = 32
ENTITIES = 131072
ALLTILES = 4096


def draw_relations(key, part):
    first = jax.random.fold_in(jax.random.fold_in(key, 11), 0)
    return jax.random.normal(first, (RELS, D), jnp.float32) * 1.2


def draw_matching(key, part):
    first, second = jax.random.split(jax.random.fold_in(key, 37))
    order = jax.random.permutation(first, GROUPS).astype(jnp.int32)
    if GROUPS <= 2:
        return order
    chosen = jax.random.randint(second, (), 0, GROUPS).astype(jnp.int32)
    target = (chosen + GROUPS // 2) % GROUPS
    places = jnp.arange(GROUPS, dtype=jnp.int32)
    holder = jnp.sum(jnp.where(order == target, places, 0)).astype(jnp.int32)
    old_value = jnp.sum(jnp.where(places == chosen, order, 0)).astype(jnp.int32)
    swapped = jnp.where(places == holder, old_value, order)
    swapped = jnp.where(places == chosen, target, swapped)
    return swapped.astype(jnp.int32)


def draw_tile_count(key, part):
    first, second = jax.random.split(jax.random.fold_in(key, 23))
    raw_draw = jax.random.randint(first, (GROUPS * MEMBERS,), 0, TILES)
    counts = 1 + raw_draw * raw_draw // TILES
    chosen = jax.random.randint(second, (), 0, GROUPS * MEMBERS)
    counts = jnp.where(jnp.arange(GROUPS * MEMBERS) == chosen, TILES, counts)
    return counts.reshape(GROUPS, MEMBERS).astype(jnp.int32)


def set_ends(entries, stream_key, low, largest):
    place = [jax.random.randint(jax.random.fold_in(stream_key, axis), (), 0, length) for axis, length in enumerate(entries.shape)]
    widest = entries.shape.index(max(entries.shape))
    beside = place[:widest] + [(place[widest] + 1) % entries.shape[widest]] + place[widest + 1:]
    return entries.at[tuple(place)].set(low).at[tuple(beside)].set(largest)


def block_scale(key, shape, shards, least, high):
    factor_of, own = 1.0, jax.random.fold_in(key, 6)
    for position, blocks in shards:
        steps = jnp.exp(jax.random.uniform(jax.random.fold_in(own, position), (blocks,), jnp.float32, least / len(shards), high / len(shards)))
        factor_of = factor_of * jnp.repeat(steps, shape[position] // blocks).reshape([-1 if axis == position else 1 for axis in range(len(shape))])
    return factor_of


def gaussian(key, shape, scale, bound, shards=(), kind=jnp.bfloat16):
    gain = block_scale(key, shape, shards, -0.22, 0.18) if shards else 1.0
    drawn = jax.random.normal(key, shape, jnp.float32) * scale * gain
    return jnp.minimum(jnp.maximum(drawn, -bound), bound).astype(kind)


def setup_inputs(seed: int = 0) -> dict:
    keys = jax.random.split(jax.random.key(seed), 9)
    return {
        "entities": gaussian(keys[0], (ENTITIES, D), 0.3, 1.796875, ((0, 256),)),
        "hub_rows": gaussian(keys[1], (HUB, D), 0.3, 1.796875),
        "relations": draw_relations(jax.random.fold_in(keys[8], 71), 0),
        "matching": draw_matching(jax.random.fold_in(keys[8], 71), 0),
        "head_index": set_ends(jax.random.randint(keys[4], (ALLTILES, EDGE), 0, ROWS), jax.random.fold_in(keys[4], 1), 0, ROWS - 1).astype(jnp.int32),
        "tail_index": set_ends(jax.random.randint(keys[5], (ALLTILES, EDGE), 0, ROWS + HUB), jax.random.fold_in(keys[5], 1), 0, (ROWS + HUB) - 1).astype(jnp.int32),
        "tile_rel": set_ends(jax.random.randint(keys[6], (ALLTILES,), 0, RELS), jax.random.fold_in(keys[6], 1), 0, RELS - 1).astype(jnp.int32),
        "tile_count": draw_tile_count(jax.random.fold_in(keys[8], 71), 0),
    }


learn_rate = 0.1


def rotate(rows, weight):
    half = rows.shape[1] // 2
    real_part = rows[:, :half]
    imag_part = rows[:, half:]
    w_real = weight[:half]
    w_imag = weight[half:]
    return jnp.concatenate([real_part * w_real - imag_part * w_imag, real_part * w_imag + imag_part * w_real], axis=1)


def pullback(grads, weight):
    half = grads.shape[1] // 2
    d_real = grads[:, :half]
    d_imag = grads[:, half:]
    w_real = weight[:half]
    w_imag = weight[half:]
    return jnp.concatenate([d_real * w_real + d_imag * w_imag, d_imag * w_real - d_real * w_imag], axis=1)


def tile_grads(head_pick, tail_pick, weight):
    query = rotate(head_pick.astype(jnp.float32), weight).astype(jnp.bfloat16)
    scores = jnp.dot(query, tail_pick.T, preferred_element_type=jnp.float32)
    top_score = jnp.max(scores, axis=1, keepdims=True)
    expo = jnp.exp(scores - top_score)
    probs = expo / jnp.sum(expo, axis=1, keepdims=True)
    diff = (probs - jnp.eye(scores.shape[0], dtype=jnp.float32)).astype(jnp.bfloat16)
    d_query = jnp.dot(diff, tail_pick, preferred_element_type=jnp.float32)
    d_tail = jnp.dot(diff.T, query, preferred_element_type=jnp.float32).astype(jnp.bfloat16)
    d_head = pullback(d_query, weight).astype(jnp.bfloat16)
    return d_head, d_tail


def reference(entities, hub_rows, relations, matching, head_index, tail_index, tile_rel, tile_count):
    blocks = entities.reshape(GROUPS, MEMBERS, ROWS, D)

    def device_grads(device):
        group_pos = device // MEMBERS
        member_pos = device % MEMBERS
        own_rows = blocks[group_pos, member_pos]
        partner = matching[group_pos]
        table = jnp.concatenate([blocks[partner, member_pos], hub_rows], axis=0)
        heads_dev = lax.dynamic_slice_in_dim(head_index, (device * TILES).astype(jnp.int32), TILES, 0)
        tails_dev = lax.dynamic_slice_in_dim(tail_index, (device * TILES).astype(jnp.int32), TILES, 0)
        rels_dev = lax.dynamic_slice_in_dim(tile_rel, (device * TILES).astype(jnp.int32), TILES, 0)
        tile_total = tile_count[group_pos, member_pos]

        def one_tile(tile_pos, grads):
            head_ids = heads_dev[tile_pos]
            tail_ids = tails_dev[tile_pos]
            weight = relations[rels_dev[tile_pos]]
            d_head, d_tail = tile_grads(own_rows[head_ids], table[tail_ids], weight)
            head_acc = grads[0] + jax.ops.segment_sum(d_head.astype(jnp.float32), head_ids, num_segments=ROWS)
            tail_acc = grads[1] + jax.ops.segment_sum(d_tail.astype(jnp.float32), tail_ids, num_segments=ROWS + HUB)
            return (head_acc, tail_acc)

        start_grads = (jnp.zeros((ROWS, D), jnp.float32), jnp.zeros((ROWS + HUB, D), jnp.float32))
        return lax.fori_loop(0, tile_total, one_tile, start_grads)

    head_grads, tail_grads = lax.map(device_grads, jnp.arange(GROUPS * MEMBERS, dtype=jnp.int32))
    back = tail_grads[:, :ROWS].astype(jnp.bfloat16).reshape(GROUPS, MEMBERS, ROWS, D)
    returned = jnp.zeros_like(back).at[matching].set(back)
    total = head_grads.reshape(GROUPS, MEMBERS, ROWS, D) + returned.astype(jnp.float32)
    new_entities = (blocks.astype(jnp.float32) - learn_rate * total).astype(jnp.bfloat16).reshape(ENTITIES, D)
    hub_grad = jnp.sum(tail_grads[:, ROWS:], axis=0)
    new_hub = (hub_rows.astype(jnp.float32) - learn_rate * hub_grad).astype(jnp.bfloat16)
    return (new_entities, new_hub)
```

```python
import jax
import jax.numpy as jnp
from jax import lax
from jax.experimental import pallas as pl
from jax.experimental.pallas import tpu as pltpu
from jax.sharding import PartitionSpec as P

learn_rate = 0.1
BF = jnp.bfloat16
F32 = jnp.float32
LANES = 128
VMEM = pl.BlockSpec(memory_space=pltpu.VMEM)
SMEM = pl.BlockSpec(memory_space=pltpu.SMEM)


def hot(ids_ref, tile, rows):
    ids = ids_ref[pl.ds(tile, 1), :]
    row = lax.broadcasted_iota(jnp.int32, (rows, ids.shape[1]), 0)
    return jnp.where(row == ids, 1.0, 0.0).astype(BF)


def pick_lane(block, lane):
    lanes = lax.broadcasted_iota(jnp.int32, block.shape, 1)
    return jnp.sum(jnp.where(lanes == lane, block, 0.0), axis=1, keepdims=True)


def dot_nn(a, b):
    return lax.dot_general(a, b, (((1,), (0,)), ((), ())), preferred_element_type=F32)


def dot_nt(a, b):
    return lax.dot_general(a, b, (((1,), (1,)), ((), ())), preferred_element_type=F32)


def dot_tn(a, b):
    return lax.dot_general(a, b, (((0,), (0,)), ((), ())), preferred_element_type=F32)


def query_kernel(count, rel_ids, ent, rel, heads, query, weights, block):
    half = ent.shape[0] // 2
    rels = rel.shape[1]
    whole = rels // LANES
    rest = rels - whole * LANES
    weights[...] = jnp.zeros_like(weights)
    block[...] = jnp.zeros_like(block)

    @pl.loop(0, count[0, 0])
    def _(tile):
        rid = rel_ids[tile]
        at = rid // LANES

        @pl.when(at < whole)
        def _():
            block[...] = rel[:, pl.ds(pl.multiple_of(at * LANES, LANES), LANES)]

        if rest:

            @pl.when(at >= whole)
            def _():
                block[:, :rest] = rel[:, whole * LANES :]

        w = pick_lane(block[...], rid - at * LANES)
        lanes = lax.broadcasted_iota(jnp.int32, weights.shape, 1)
        weights[...] = jnp.where(lanes == tile, w, weights[...])
        head = dot_nn(ent[...], hot(heads, tile, ent.shape[1]))
        hr, hi = head[:half], head[half:]
        wr, wi = w[:half], w[half:]
        query[tile] = jnp.concatenate([hr * wr - hi * wi, hr * wi + hi * wr], axis=0).astype(BF)


def tail_kernel(count, query, partner, hub, tails, pick, diff, grads, table, acc):
    dim, rows = hub.shape[0], partner.shape[1]
    table[:, :rows] = partner[:dim]
    table[:, rows:] = hub[...]
    acc[...] = jnp.zeros_like(acc)

    @pl.loop(0, count[0, 0])
    def _(tile):
        tail_hot = hot(tails, tile, table.shape[1])
        tail = dot_nn(table[...], tail_hot).astype(BF)
        pick[tile] = tail
        q = query[tile]
        scores = dot_tn(tail, q)
        top = jnp.max(scores, axis=0, keepdims=True)
        expo = jnp.exp(scores - top)
        probs = expo * (1.0 / jnp.sum(expo, axis=0, keepdims=True))
        eye = lax.broadcasted_iota(jnp.int32, scores.shape, 0) == lax.broadcasted_iota(
            jnp.int32, scores.shape, 1
        )
        d = (probs - jnp.where(eye, 1.0, 0.0)).astype(BF)
        diff[tile] = d
        d_tail = dot_nt(q, d).astype(BF)
        acc[...] += dot_nt(d_tail, tail_hot)

    chunks, step = grads.shape[0], grads.shape[1]
    for c in range(chunks):
        n = min(step, dim - c * step)
        grads[c, :n] = acc[c * step : c * step + n].astype(BF)
        if n < step:
            grads[c, n:] = jnp.zeros((step - n, grads.shape[2]), BF)


def head_kernel(count, pick, diff, weights, heads, acc):
    half = acc.shape[0] // 2
    acc[...] = jnp.zeros_like(acc)

    @pl.loop(0, count[0, 0])
    def _(tile):
        d_query = dot_nn(pick[tile], diff[tile])
        w = pick_lane(weights[...], tile)
        dr, di = d_query[:half], d_query[half:]
        wr, wi = w[:half], w[half:]
        d_head = jnp.concatenate([dr * wr + di * wi, di * wr - dr * wi], axis=0).astype(BF)
        acc[...] += dot_nt(d_head, hot(heads, tile, acc.shape[1]))


def reorder_kernel(matching, rows, out):
    for g in range(out.shape[0]):
        out[g] = rows[matching[g]]


def return_kernel(matching, back, hub, out):
    rows = out.shape[2] - hub.shape[2]
    total = hub[0].astype(F32)
    for m in range(1, hub.shape[0]):
        total += hub[m].astype(F32)
    total = total.astype(BF)
    for g in range(out.shape[0]):
        out[matching[g], :, :rows] = back[g, :, :rows]
        out[g, :, rows:] = total


def call(kernel, out_shape, in_specs, flops, moved, scratch=(), exps=0):
    many = isinstance(out_shape, (list, tuple))
    return pl.pallas_call(
        kernel,
        out_shape=out_shape,
        in_specs=in_specs,
        out_specs=[VMEM] * len(out_shape) if many else VMEM,
        scratch_shapes=scratch,
        compiler_params=pltpu.CompilerParams(vmem_limit_bytes=32 * 1024 * 1024),
        cost_estimate=pl.CostEstimate(flops=flops, bytes_accessed=moved, transcendentals=exps),
    )


def make(groups, members):
    def shards(entities, hub_rows, relations, matching, head_index, tail_index, tile_rel, tile_count):
        ent, hub, rel = entities.T, hub_rows.T, relations.T
        dim, rows = ent.shape
        hubs = hub.shape[1]
        tiles, edges = head_index.shape
        step = -(-dim // (8 * groups)) * 8
        shape = jax.ShapeDtypeStruct

        cut = jnp.pad(ent, ((0, groups * step - dim), (0, 0))).reshape(groups, step, rows)
        cut = lax.all_to_all(cut, "group", 0, 0)
        cut = call(
            reorder_kernel, shape(cut.shape, BF), [SMEM, VMEM], 0, 4 * cut.size
        )(matching, cut)
        partner = lax.all_to_all(cut, "group", 0, 0).reshape(groups * step, rows)

        one = 2 * tiles * edges * dim
        query, weights = call(
            query_kernel,
            [shape((tiles, dim, edges), BF), shape((dim, LANES), F32)],
            [SMEM, SMEM, VMEM, VMEM, VMEM],
            one * rows,
            8 * rel.size,
            [pltpu.VMEM((dim, LANES), F32)],
        )(tile_count, tile_rel, ent, rel, head_index)
        pick, diff, grads = call(
            tail_kernel,
            [
                shape((tiles, dim, edges), BF),
                shape((tiles, edges, edges), BF),
                shape((groups, step, rows + hubs), BF),
            ],
            [SMEM, VMEM, VMEM, VMEM, VMEM],
            2 * one * (rows + hubs + edges),
            8 * tiles * dim * edges,
            [pltpu.VMEM((dim, rows + hubs), BF), pltpu.VMEM((dim, rows + hubs), F32)],
            tiles * edges * edges,
        )(tile_count, query, partner, hub, tail_index)
        head_acc = call(
            head_kernel,
            shape((dim, rows), F32),
            [SMEM, VMEM, VMEM, VMEM, VMEM],
            one * (rows + edges),
            6 * tiles * dim * edges,
        )(tile_count, pick, diff, weights, head_index)

        got = lax.all_to_all(grads, "group", 0, 0)
        part = jnp.sum(got[:, :, rows:].astype(F32), axis=0).astype(BF)
        parts = jnp.broadcast_to(part[None], (members,) + part.shape)
        parts = lax.all_to_all(parts, "member", 0, 0)
        sent = call(
            return_kernel, shape(got.shape, BF), [SMEM, VMEM, VMEM], 0, 4 * got.size
        )(matching, got, parts)
        last = lax.all_to_all(sent, "group", 0, 0).reshape(groups * step, rows + hubs)[:dim].astype(F32)
        new_entities = (ent.astype(F32) - learn_rate * (head_acc + last[:, :rows])).astype(BF)
        new_hub = (hub.astype(F32) - learn_rate * last[:, rows:]).astype(BF)
        return (new_entities.T, new_hub.T)

    return shards


def solution(mesh):
    placed = (
        P(("group", "member"), None),
        P(),
        P(),
        P(),
        P(("group", "member"), None),
        P(("group", "member"), None),
        P(("group", "member")),
        P("group", "member"),
    )
    return jax.shard_map(
        make(mesh.shape["group"], mesh.shape["member"]),
        mesh=mesh,
        in_specs=placed,
        out_specs=(P(("group", "member"), None), P()),
        check_vma=False,
    )
```

```python
import jax
import jax.numpy as jnp
from jax import lax
from jax.experimental import pallas as pl
from jax.experimental.pallas import tpu as pltpu
from jax.sharding import PartitionSpec as P

learn_rate = 0.1
BF = jnp.bfloat16
F32 = jnp.float32
LANES = 128
VMEM = pl.BlockSpec(memory_space=pltpu.VMEM)
SMEM = pl.BlockSpec(memory_space=pltpu.SMEM)
HBM = pl.BlockSpec(memory_space=pltpu.HBM)
DMA = pltpu.SemaphoreType.DMA


def hot(ids, rows):
    row = lax.broadcasted_iota(jnp.int32, (rows, ids.shape[1]), 0)
    return jnp.where(row == ids, 1.0, 0.0).astype(BF)


def pair_ids(ids_ref, pair):
    return jnp.concatenate([ids_ref[pl.ds(2 * pair, 1), :], ids_ref[pl.ds(2 * pair + 1, 1), :]], axis=1)


def pick_lane(block, lane):
    lanes = lax.broadcasted_iota(jnp.int32, block.shape, 1)
    return jnp.sum(jnp.where(lanes == lane, block, 0.0), axis=1, keepdims=True)


def dot_nn(a, b):
    return lax.dot_general(a, b, (((1,), (0,)), ((), ())), preferred_element_type=F32)


def dot_nt(a, b):
    return lax.dot_general(a, b, (((1,), (1,)), ((), ())), preferred_element_type=F32)


def dot_tn(a, b):
    return lax.dot_general(a, b, (((0,), (0,)), ((), ())), preferred_element_type=F32)


def query_kernel(count, rel_ids, ent, rel, heads, query, weights, block, out, sems):
    half = ent.shape[0] // 2
    edges = query.shape[2]
    whole = rel.shape[1] // LANES
    rest = rel.shape[1] - whole * LANES
    live = count[0, 0]
    pairs = (live + 1) // 2
    weights[...] = jnp.zeros_like(weights)
    block[...] = jnp.zeros_like(block)

    def copy(pair):
        slot = pair % 2
        return pltpu.make_async_copy(out.at[slot], query.at[pl.ds(2 * pair, 2)], sems.at[slot])

    @pl.loop(0, pairs)
    def _(pair):
        @pl.when(pair >= 2)
        def _():
            copy(pair - 2).wait()

        for k in range(2):
            at = rel_ids[2 * pair + k] // LANES

            @pl.when(at < whole)
            def _():
                block[k] = rel[:, pl.ds(pl.multiple_of(at * LANES, LANES), LANES)]

            if rest:

                @pl.when(at >= whole)
                def _():
                    block[k, :, :rest] = rel[:, whole * LANES :]

        head = dot_nn(ent[...], hot(pair_ids(heads, pair), ent.shape[1]))
        for k in range(2):
            tile = 2 * pair + k
            rid = rel_ids[tile]
            w = pick_lane(block[k], rid - rid // LANES * LANES)
            w = jnp.where(tile < live, w, 0.0)
            lanes = lax.broadcasted_iota(jnp.int32, weights.shape, 1)
            weights[...] = jnp.where(lanes == tile, w, weights[...])
            hr = head[:half, k * edges : (k + 1) * edges]
            hi = head[half:, k * edges : (k + 1) * edges]
            wr, wi = w[:half], w[half:]
            out[pair % 2, k] = jnp.concatenate(
                [hr * wr - hi * wi, hr * wi + hi * wr], axis=0
            ).astype(BF)
        copy(pair).start()

    @pl.when(pairs >= 2)
    def _():
        copy(pairs - 2).wait()

    copy(pairs - 1).wait()


def tail_kernel(count, query, partner, hub, tails, pick, diff, grads, table, acc, qin, pout, dout, qsem, psem, dsem):
    dim, rows = hub.shape[0], partner.shape[1]
    edges = tails.shape[1]
    live = count[0, 0]
    pairs = (live + 1) // 2

    def fetch(pair):
        slot = pair % 2
        return pltpu.make_async_copy(query.at[pl.ds(2 * pair, 2)], qin.at[slot], qsem.at[slot])

    def put_pick(pair):
        slot = pair % 2
        return pltpu.make_async_copy(pout.at[slot], pick.at[pair], psem.at[slot])

    def put_diff(pair):
        slot = pair % 2
        return pltpu.make_async_copy(dout.at[slot], diff.at[pl.ds(2 * pair, 2)], dsem.at[slot])

    fetch(0).start()
    table[:, :rows] = partner[:dim]
    table[:, rows:] = hub[...]
    acc[...] = jnp.zeros_like(acc)
    eye = lax.broadcasted_iota(jnp.int32, (edges, edges), 0) == lax.broadcasted_iota(
        jnp.int32, (edges, edges), 1
    )

    @pl.loop(0, pairs)
    def _(pair):
        slot = pair % 2
        fetch(pair).wait()

        @pl.when(pair + 1 < pairs)
        def _():
            fetch(pair + 1).start()

        @pl.when(pair >= 2)
        def _():
            put_pick(pair - 2).wait()
            put_diff(pair - 2).wait()

        tail_hot = hot(pair_ids(tails, pair), table.shape[1])
        both = dot_nn(table[...], tail_hot).astype(BF)
        pout[slot] = both
        d_tails = []
        for k in range(2):
            q = qin[slot, k]
            tail = both[:, k * edges : (k + 1) * edges]
            scores = dot_tn(tail, q)
            top = jnp.max(scores, axis=0, keepdims=True)
            expo = jnp.exp(scores - top)
            probs = expo * (1.0 / jnp.sum(expo, axis=0, keepdims=True))
            d = jnp.where(eye, probs - 1.0, probs)
            if k:
                d = jnp.where(2 * pair + 1 < live, d, 0.0)
            d = d.astype(BF)
            dout[slot, k] = d
            d_tails.append(dot_nt(q, d).astype(BF))
        acc[...] += dot_nt(jnp.concatenate(d_tails, axis=1), tail_hot)
        put_pick(pair).start()
        put_diff(pair).start()

    chunks, step = grads.shape[0], grads.shape[1]
    for c in range(chunks):
        n = min(step, dim - c * step)
        grads[c, :n] = acc[c * step : c * step + n].astype(BF)
        if n < step:
            grads[c, n:] = jnp.zeros((step - n, grads.shape[2]), BF)

    @pl.when(pairs >= 2)
    def _():
        put_pick(pairs - 2).wait()
        put_diff(pairs - 2).wait()

    put_pick(pairs - 1).wait()
    put_diff(pairs - 1).wait()


def head_kernel(count, pick, diff, weights, heads, acc, pin, din, psem, dsem):
    half = acc.shape[0] // 2
    edges = heads.shape[1]
    live = count[0, 0]
    pairs = (live + 1) // 2

    def get_pick(pair):
        slot = pair % 2
        return pltpu.make_async_copy(pick.at[pair], pin.at[slot], psem.at[slot])

    def get_diff(pair):
        slot = pair % 2
        return pltpu.make_async_copy(diff.at[pl.ds(2 * pair, 2)], din.at[slot], dsem.at[slot])

    get_pick(0).start()
    get_diff(0).start()
    acc[...] = jnp.zeros_like(acc)

    @pl.loop(0, pairs)
    def _(pair):
        slot = pair % 2
        get_pick(pair).wait()
        get_diff(pair).wait()

        @pl.when(pair + 1 < pairs)
        def _():
            get_pick(pair + 1).start()
            get_diff(pair + 1).start()

        d_heads = []
        for k in range(2):
            d_query = dot_nn(pin[slot, :, k * edges : (k + 1) * edges], din[slot, k])
            w = pick_lane(weights[...], 2 * pair + k)
            dr, di = d_query[:half], d_query[half:]
            wr, wi = w[:half], w[half:]
            d_heads.append(
                jnp.concatenate([dr * wr + di * wi, di * wr - dr * wi], axis=0).astype(BF)
            )
        head_hot = hot(pair_ids(heads, pair), acc.shape[1])
        acc[...] += dot_nt(jnp.concatenate(d_heads, axis=1), head_hot)


def reorder_kernel(matching, rows, out):
    for g in range(out.shape[0]):
        out[g] = rows[matching[g]]


def return_kernel(matching, back, hub, out):
    rows = out.shape[2] - hub.shape[2]
    total = hub[0].astype(F32)
    for m in range(1, hub.shape[0]):
        total += hub[m].astype(F32)
    total = total.astype(BF)
    for g in range(out.shape[0]):
        out[matching[g], :, :rows] = back[g, :, :rows]
        out[g, :, rows:] = total


def update_kernel(ent, hub, head_acc, last, new_ent, new_hub):
    dim, rows = ent.shape
    step = last.shape[1]
    for c in range(last.shape[0]):
        n = min(step, dim - c * step)
        at = slice(c * step, c * step + n)
        got = last[c, :n].astype(F32)
        new_ent[at] = (ent[at].astype(F32) - learn_rate * (head_acc[at] + got[:, :rows])).astype(BF)
        new_hub[at] = (hub[at].astype(F32) - learn_rate * got[:, rows:]).astype(BF)


def call(kernel, out_shape, in_specs, out_specs, flops, moved, scratch=(), exps=0, vmem=32):
    return pl.pallas_call(
        kernel,
        out_shape=out_shape,
        in_specs=in_specs,
        out_specs=out_specs,
        scratch_shapes=scratch,
        compiler_params=pltpu.CompilerParams(vmem_limit_bytes=vmem * 1024 * 1024),
        cost_estimate=pl.CostEstimate(flops=flops, bytes_accessed=moved, transcendentals=exps),
    )


shape = jax.ShapeDtypeStruct


def run_query(tile_count, tile_rel, ent, rel, head_index):
    dim, rows = ent.shape
    tiles, edges = head_index.shape
    return call(
        query_kernel,
        [shape((tiles, dim, edges), BF), shape((dim, LANES), F32)],
        [SMEM, SMEM, VMEM, VMEM, VMEM],
        [HBM, VMEM],
        2 * tiles * edges * dim * rows,
        8 * rel.size,
        [pltpu.VMEM((2, dim, LANES), F32), pltpu.VMEM((2, 2, dim, edges), BF), DMA((2,))],
        vmem=58,
    )(tile_count, tile_rel, ent, rel, head_index)


def run_tail(tile_count, query, partner, hub, tail_index, groups, step):
    tiles, dim, edges = query.shape
    rows, hubs = partner.shape[1], hub.shape[1]
    return call(
        tail_kernel,
        [
            shape((tiles // 2, dim, 2 * edges), BF),
            shape((tiles, edges, edges), BF),
            shape((groups, step, rows + hubs), BF),
        ],
        [SMEM, HBM, VMEM, VMEM, VMEM],
        [HBM, HBM, VMEM],
        4 * tiles * edges * dim * (rows + hubs + edges),
        8 * tiles * dim * edges,
        [
            pltpu.VMEM((dim, rows + hubs), BF),
            pltpu.VMEM((dim, rows + hubs), F32),
            pltpu.VMEM((2, 2, dim, edges), BF),
            pltpu.VMEM((2, dim, 2 * edges), BF),
            pltpu.VMEM((2, 2, edges, edges), BF),
            DMA((2,)),
            DMA((2,)),
            DMA((2,)),
        ],
        tiles * edges * edges,
        vmem=61,
    )(tile_count, query, partner, hub, tail_index)


def run_head(tile_count, pick, diff, weights, head_index, rows):
    pairs, dim, wide = pick.shape
    edges = wide // 2
    return call(
        head_kernel,
        shape((dim, rows), F32),
        [SMEM, HBM, HBM, VMEM, VMEM],
        VMEM,
        4 * pairs * edges * dim * (rows + edges),
        12 * pairs * dim * edges,
        [
            pltpu.VMEM((2, dim, wide), BF),
            pltpu.VMEM((2, 2, edges, edges), BF),
            DMA((2,)),
            DMA((2,)),
        ],
        vmem=61,
    )(tile_count, pick, diff, weights, head_index)


def make(groups, members):
    def shards(entities, hub_rows, relations, matching, head_index, tail_index, tile_rel, tile_count):
        ent, hub, rel = entities.T, hub_rows.T, relations.T
        dim, rows = ent.shape
        hubs = hub.shape[1]
        step = -(-dim // (8 * groups)) * 8

        cut = jnp.pad(ent, ((0, groups * step - dim), (0, 0))).reshape(groups, step, rows)
        cut = lax.all_to_all(cut, "group", 0, 0)
        query, weights = run_query(tile_count, tile_rel, ent, rel, head_index)
        cut, query, weights = lax.optimization_barrier((cut, query, weights))
        cut = call(reorder_kernel, shape(cut.shape, BF), [SMEM, VMEM], VMEM, 0, 4 * cut.size)(
            matching, cut
        )
        partner = lax.all_to_all(cut, "group", 0, 0).reshape(groups * step, rows)
        pick, diff, grads = run_tail(tile_count, query, partner, hub, tail_index, groups, step)

        got = lax.all_to_all(grads, "group", 0, 0)
        got, pick, diff = lax.optimization_barrier((got, pick, diff))
        part = jnp.sum(got[:, :, rows:].astype(F32), axis=0).astype(BF)
        parts = jnp.broadcast_to(part[None], (members,) + part.shape)
        parts = lax.all_to_all(parts, "member", 0, 0)
        head_acc = run_head(tile_count, pick, diff, weights, head_index, rows)
        parts, head_acc = lax.optimization_barrier((parts, head_acc))
        sent = call(
            return_kernel, shape(got.shape, BF), [SMEM, VMEM, VMEM], VMEM, 0, 4 * got.size
        )(matching, got, parts)
        last = lax.all_to_all(sent, "group", 0, 0)
        new_ent, new_hub = call(
            update_kernel,
            [shape((dim, rows), BF), shape((dim, hubs), BF)],
            [VMEM, VMEM, VMEM, VMEM],
            [VMEM, VMEM],
            0,
            8 * dim * rows,
        )(ent, hub, head_acc, last)
        return (new_ent.T, new_hub.T)

    return shards


def solution(mesh):
    placed = (
        P(("group", "member"), None),
        P(),
        P(),
        P(),
        P(("group", "member"), None),
        P(("group", "member"), None),
        P(("group", "member")),
        P("group", "member"),
    )
    return jax.shard_map(
        make(mesh.shape["group"], mesh.shape["member"]),
        mesh=mesh,
        in_specs=placed,
        out_specs=(P(("group", "member"), None), P()),
        check_vma=False,
    )
```

```python
import jax
import jax.numpy as jnp
from jax import lax
from jax.experimental import pallas as pl
from jax.experimental.pallas import tpu as pltpu
from jax.sharding import PartitionSpec as P

learn_rate = 0.1
BF = jnp.bfloat16
F32 = jnp.float32
LANES = 128
VMEM = pl.BlockSpec(memory_space=pltpu.VMEM)
SMEM = pl.BlockSpec(memory_space=pltpu.SMEM)
HBM = pl.BlockSpec(memory_space=pltpu.HBM)
DMA = pltpu.SemaphoreType.DMA


def hot(ids, rows):
    row = lax.broadcasted_iota(jnp.int32, (rows, ids.shape[1]), 0)
    return jnp.where(row == ids, 1.0, 0.0).astype(BF)


def pair_ids(ids_ref, pair):
    return jnp.concatenate([ids_ref[pl.ds(2 * pair, 1), :], ids_ref[pl.ds(2 * pair + 1, 1), :]], axis=1)


def pick_lane(block, lane):
    lanes = lax.broadcasted_iota(jnp.int32, block.shape, 1)
    return jnp.sum(jnp.where(lanes == lane, block, 0.0), axis=1, keepdims=True)


def dot_nn(a, b):
    return lax.dot_general(a, b, (((1,), (0,)), ((), ())), preferred_element_type=F32)


def dot_nt(a, b):
    return lax.dot_general(a, b, (((1,), (1,)), ((), ())), preferred_element_type=F32)


def dot_tn(a, b):
    return lax.dot_general(a, b, (((0,), (0,)), ((), ())), preferred_element_type=F32)


def rotate_pair(pair, live, ent, heads, weights, out):
    half, edges = ent.shape[0] // 2, heads.shape[1]
    head = dot_nn(ent[...], hot(pair_ids(heads, pair), ent.shape[1]))
    for k in range(2):
        w = pick_lane(weights[...], 2 * pair + k)
        hr = head[:half, k * edges : (k + 1) * edges]
        hi = head[half:, k * edges : (k + 1) * edges]
        wr, wi = w[:half], w[half:]
        out[k] = jnp.concatenate([hr * wr - hi * wi, hr * wi + hi * wr], axis=0).astype(BF)


def first_kernel(count, rel_ids, ent, rel, heads, query, weights, table, block, out, rel_sem, sem):
    live = count[0, 0]
    whole = rel.shape[1] // LANES
    rest = rel.shape[1] - whole * LANES
    load = pltpu.make_async_copy(rel, table, rel_sem)
    load.start()
    weights[...] = jnp.zeros_like(weights)
    block[...] = jnp.zeros_like(block)
    load.wait()

    @pl.loop(0, (live + 1) // 2)
    def _(pair):
        for k in range(2):
            at = rel_ids[2 * pair + k] // LANES

            @pl.when(at < whole)
            def _():
                block[k] = table[:, pl.ds(pl.multiple_of(at * LANES, LANES), LANES)]

            if rest:

                @pl.when(at >= whole)
                def _():
                    block[k, :, :rest] = table[:, whole * LANES :]

        total = weights[...]
        lanes = lax.broadcasted_iota(jnp.int32, weights.shape, 1)
        for k in range(2):
            tile = 2 * pair + k
            rid = rel_ids[tile]
            w = pick_lane(block[k], rid - rid // LANES * LANES)
            w = jnp.where(tile < live, w, 0.0)
            total = jnp.where(lanes == tile, w, total)
        weights[...] = total

    rotate_pair(0, live, ent, heads, weights, out)
    put = pltpu.make_async_copy(out, query.at[pl.ds(0, 2)], sem)
    put.start()
    put.wait()


def query_kernel(count, ent, heads, weights, begun, query, out, sems):
    live = count[0, 0]
    pairs = 2 * ((live + 3) // 4)

    def put(pair):
        return pltpu.make_async_copy(out.at[pair], query.at[pl.ds(2 * pair, 2)], sems.at[pair])

    @pl.loop(1, pairs)
    def _(pair):
        rotate_pair(pair, live, ent, heads, weights, out.at[pair])
        put(pair).start()

    @pl.loop(1, pairs)
    def _(pair):
        put(pair).wait()


def tail_kernel(count, query, partner, hub, tails, pick, diff, grads, table, acc, qin, picks, diffs, moves, qsem, psem, dsem):
    dim, rows = hub.shape[0], partner.shape[1]
    edges = tails.shape[1]
    live = count[0, 0]
    quads = (live + 3) // 4
    pairs = 2 * quads

    def fetch(pair):
        both = pl.ds(2 * pair, 2)
        return pltpu.make_async_copy(query.at[both], qin.at[both], qsem.at[pair])

    def put_pick(pair, slot):
        return pltpu.make_async_copy(picks.at[slot], pick.at[pair], psem.at[slot])

    def put_diff(pair):
        both = pl.ds(2 * pair, 2)
        return pltpu.make_async_copy(diffs.at[both], diff.at[both], dsem.at[pair])

    @pl.loop(0, pairs)
    def _(pair):
        fetch(pair).start()

    table[:, :rows] = partner[:dim]
    table[:, rows:] = hub[...]
    acc[...] = jnp.zeros_like(acc)
    moves[...] = jnp.zeros_like(moves)
    eye = lax.broadcasted_iota(jnp.int32, (edges, edges), 0) == lax.broadcasted_iota(
        jnp.int32, (edges, edges), 1
    )

    def pick_tails(pair, slot):
        picks[slot] = dot_nn(table[...], hot(pair_ids(tails, pair), table.shape[1])).astype(BF)

    def spread(pair, slot):
        acc[...] += dot_nt(moves[slot], hot(pair_ids(tails, pair), table.shape[1]))

    pick_tails(0, 0)
    put_pick(0, 0).start()

    @pl.loop(0, quads)
    def _(quad):
        for slot in range(2):
            pair = 2 * quad + slot
            fetch(pair).wait()

            @pl.when(pair >= 1)
            def _():
                put_pick(pair - 1, 1 - slot).wait()

            ats = [slice(k * edges, (k + 1) * edges) for k in range(2)]
            qs = [qin[2 * pair + k] for k in range(2)]
            scores = [dot_tn(picks[slot, :, ats[k]], qs[k]) for k in range(2)]
            spread(jnp.maximum(pair - 1, 0), 1 - slot)
            ds = []
            for k in range(2):
                tile = 2 * pair + k
                top = jnp.max(scores[k], axis=0, keepdims=True)
                expo = jnp.exp(scores[k] - top)
                probs = expo * (1.0 / jnp.sum(expo, axis=0, keepdims=True))
                d = jnp.where(eye, probs - 1.0, probs)
                if slot + k:
                    d = jnp.where(tile < live, d, 0.0)
                ds.append(d.astype(BF))
                diffs[tile] = ds[k]
            pick_tails(jnp.minimum(pair + 1, pairs - 1), 1 - slot)
            for k in range(2):
                moves[slot, :, ats[k]] = dot_nt(qs[k], ds[k]).astype(BF)
            put_diff(pair).start()

            @pl.when(pair + 1 < pairs)
            def _():
                put_pick(pair + 1, 1 - slot).start()

    spread(pairs - 1, 1)
    chunks, step = grads.shape[0], grads.shape[1]
    for c in range(chunks):
        n = min(step, dim - c * step)
        grads[c, :n] = acc[c * step : c * step + n].astype(BF)
        if n < step:
            grads[c, n:] = jnp.zeros((step - n, grads.shape[2]), BF)
    put_pick(pairs - 1, 1).wait()

    @pl.loop(0, pairs)
    def _(pair):
        put_diff(pair).wait()


def head_kernel(count, pick, diff, weights, heads, acc, pin, din, moves, psem, dsem):
    half = acc.shape[0] // 2
    edges = heads.shape[1]
    live = count[0, 0]
    quads = (live + 3) // 4
    pairs = 2 * quads

    def get_pick(pair):
        return pltpu.make_async_copy(pick.at[pair], pin.at[pair], psem.at[pair])

    def get_diff(pair):
        both = pl.ds(2 * pair, 2)
        return pltpu.make_async_copy(diff.at[both], din.at[both], dsem.at[pair])

    @pl.loop(0, pairs)
    def _(pair):
        get_pick(pair).start()
        get_diff(pair).start()

    acc[...] = jnp.zeros_like(acc)
    moves[...] = jnp.zeros_like(moves)

    def spread(pair, slot):
        acc[...] += dot_nt(moves[slot], hot(pair_ids(heads, pair), acc.shape[1]))

    @pl.loop(0, quads)
    def _(quad):
        for slot in range(2):
            pair = 2 * quad + slot
            get_pick(pair).wait()
            get_diff(pair).wait()
            ats = [slice(k * edges, (k + 1) * edges) for k in range(2)]
            d_query = [dot_nn(pin[pair, :, ats[k]], din[2 * pair + k]) for k in range(2)]
            spread(jnp.maximum(pair - 1, 0), 1 - slot)
            for k in range(2):
                w = pick_lane(weights[...], 2 * pair + k)
                dr, di = d_query[k][:half], d_query[k][half:]
                wr, wi = w[:half], w[half:]
                moves[slot, :, ats[k]] = jnp.concatenate(
                    [dr * wr + di * wi, di * wr - dr * wi], axis=0
                ).astype(BF)

    spread(pairs - 1, 1)


def spread_kernel(rows, out, sem):
    put = pltpu.make_async_copy(rows, out.at[pl.ds(0, rows.shape[0])], sem)
    put.start()
    put.wait()


def reorder_kernel(matching, rows, out):
    for g in range(out.shape[0]):
        out[g] = rows[matching[g]]


def return_kernel(matching, back, hub, out):
    rows = out.shape[2] - hub.shape[2]
    total = hub[0].astype(F32)
    for m in range(1, hub.shape[0]):
        total += hub[m].astype(F32)
    total = total.astype(BF)
    for g in range(out.shape[0]):
        out[matching[g], :, :rows] = back[g, :, :rows]
        out[g, :, rows:] = total


def update_kernel(ent, hub, head_acc, last, new_ent, new_hub):
    dim, rows = ent.shape
    step = last.shape[1]
    for c in range(last.shape[0]):
        n = min(step, dim - c * step)
        at = slice(c * step, c * step + n)
        got = last[c, :n].astype(F32)
        new_ent[at] = (ent[at].astype(F32) - learn_rate * (head_acc[at] + got[:, :rows])).astype(BF)
        new_hub[at] = (hub[at].astype(F32) - learn_rate * got[:, rows:]).astype(BF)


def call(kernel, out_shape, in_specs, out_specs, flops, moved, scratch=(), exps=0, vmem=32, aliases={}):
    return pl.pallas_call(
        kernel,
        out_shape=out_shape,
        in_specs=in_specs,
        out_specs=out_specs,
        scratch_shapes=scratch,
        input_output_aliases=aliases,
        compiler_params=pltpu.CompilerParams(vmem_limit_bytes=vmem * 1024 * 1024),
        cost_estimate=pl.CostEstimate(flops=flops, bytes_accessed=moved, transcendentals=exps),
    )


shape = jax.ShapeDtypeStruct


def run_first(tile_count, tile_rel, ent, rel, head_index):
    dim, rows = ent.shape
    tiles, edges = head_index.shape
    return call(
        first_kernel,
        [shape((2 * tiles, dim, edges), BF), shape((dim, LANES), F32)],
        [SMEM, SMEM, VMEM, HBM, VMEM],
        [HBM, VMEM],
        4 * edges * dim * rows,
        4 * rel.size,
        [
            pltpu.VMEM(rel.shape, F32),
            pltpu.VMEM((2, dim, LANES), F32),
            pltpu.VMEM((2, dim, edges), BF),
            DMA(()),
            DMA(()),
        ],
        vmem=60,
    )(tile_count, tile_rel, ent, rel, head_index)


def run_query(tile_count, ent, head_index, weights, begun):
    dim, rows = ent.shape
    tiles, edges = head_index.shape
    return call(
        query_kernel,
        shape(begun.shape, BF),
        [SMEM, VMEM, VMEM, VMEM, HBM],
        HBM,
        2 * tiles * edges * dim * rows,
        2 * tiles * dim * edges,
        [pltpu.VMEM((tiles // 2, 2, dim, edges), BF), DMA((tiles // 2,))],
        vmem=60,
        aliases={4: 0},
    )(tile_count, ent, head_index, weights, begun)


def run_tail(tile_count, query, partner, hub, tail_index, groups, step):
    tiles, edges = tail_index.shape
    dim = query.shape[1]
    rows, hubs = partner.shape[1], hub.shape[1]
    return call(
        tail_kernel,
        [
            shape((tiles, dim, 2 * edges), BF),
            shape((3 * tiles, edges, edges), BF),
            shape((groups, step, rows + hubs), BF),
        ],
        [SMEM, HBM, VMEM, VMEM, VMEM],
        [HBM, HBM, VMEM],
        4 * tiles * edges * dim * (rows + hubs + edges),
        8 * tiles * dim * edges,
        [
            pltpu.VMEM((dim, rows + hubs), BF),
            pltpu.VMEM((dim, rows + hubs), F32),
            pltpu.VMEM((tiles, dim, edges), BF),
            pltpu.VMEM((2, dim, 2 * edges), BF),
            pltpu.VMEM((tiles, edges, edges), BF),
            pltpu.VMEM((2, dim, 2 * edges), BF),
            DMA((tiles // 2,)),
            DMA((2,)),
            DMA((tiles // 2,)),
        ],
        tiles * edges * edges,
        vmem=50,
    )(tile_count, query, partner, hub, tail_index)


def run_head(tile_count, pick, diff, weights, head_index, rows):
    tiles, edges = head_index.shape
    dim = pick.shape[1]
    return call(
        head_kernel,
        shape((dim, rows), F32),
        [SMEM, HBM, HBM, VMEM, VMEM],
        VMEM,
        2 * tiles * edges * dim * (rows + edges),
        6 * tiles * dim * edges,
        [
            pltpu.VMEM((tiles // 2, dim, 2 * edges), BF),
            pltpu.VMEM((tiles, edges, edges), BF),
            pltpu.VMEM((2, dim, 2 * edges), BF),
            DMA((tiles // 2,)),
            DMA((tiles // 2,)),
        ],
        vmem=60,
    )(tile_count, pick, diff, weights, head_index)


def make(groups, members):
    def shards(entities, hub_rows, relations, matching, head_index, tail_index, tile_rel, tile_count):
        ent, hub, rel = entities.T, hub_rows.T, relations.T
        dim, rows = ent.shape
        hubs = hub.shape[1]
        step = -(-dim // (8 * groups)) * 8

        cut = call(
            spread_kernel, shape((groups * step, rows), BF), [HBM], HBM, 0, 4 * ent.size, [DMA(())], vmem=62
        )(ent)
        cut = lax.all_to_all(cut.reshape(groups, step, rows), "group", 0, 0)
        query, weights = run_first(tile_count, tile_rel, ent, rel, head_index)
        cut, query, weights = lax.optimization_barrier((cut, query, weights))
        cut = call(reorder_kernel, shape(cut.shape, BF), [SMEM, VMEM], VMEM, 0, 4 * cut.size)(
            matching, cut
        )
        partner = lax.all_to_all(cut, "group", 0, 0).reshape(groups * step, rows)
        query = run_query(tile_count, ent, head_index, weights, query)
        pick, diff, grads = run_tail(tile_count, query, partner, hub, tail_index, groups, step)

        got = lax.all_to_all(grads, "group", 0, 0)
        got, pick, diff = lax.optimization_barrier((got, pick, diff))
        part = jnp.sum(got[:, :, rows:].astype(F32), axis=0).astype(BF)
        other = lax.ppermute(part, "member", [(m, m ^ 1) for m in range(members)])
        part = (part.astype(F32) + other.astype(F32)).astype(BF)
        cores = [list(range(core, members, 2)) for core in range(2)]
        parts = jnp.broadcast_to(part[None], (members // 2,) + part.shape)
        parts = lax.all_to_all(parts, "member", 0, 0, axis_index_groups=cores)
        head_acc = run_head(tile_count, pick, diff, weights, head_index, rows)
        parts, head_acc = lax.optimization_barrier((parts, head_acc))
        sent = call(
            return_kernel, shape(got.shape, BF), [SMEM, VMEM, VMEM], VMEM, 0, 4 * got.size
        )(matching, got, parts)
        last = lax.all_to_all(sent, "group", 0, 0)
        new_ent, new_hub = call(
            update_kernel,
            [shape((dim, rows), BF), shape((dim, hubs), BF)],
            [VMEM, VMEM, VMEM, VMEM],
            [VMEM, VMEM],
            0,
            8 * dim * rows,
        )(ent, hub, head_acc, last)
        return (new_ent.T, new_hub.T)

    return shards


def solution(mesh):
    placed = (
        P(("group", "member"), None),
        P(),
        P(),
        P(),
        P(("group", "member"), None),
        P(("group", "member"), None),
        P(("group", "member")),
        P("group", "member"),
    )
    return jax.shard_map(
        make(mesh.shape["group"], mesh.shape["member"]),
        mesh=mesh,
        in_specs=placed,
        out_specs=(P(("group", "member"), None), P()),
        check_vma=False,
    )
```

```python
import jax
import jax.numpy as jnp
from jax import lax
from jax.experimental import pallas as pl
from jax.experimental.pallas import tpu as pltpu
from jax.sharding import PartitionSpec as P

learn_rate = 0.1
BF = jnp.bfloat16
F32 = jnp.float32
LANES = 128
VMEM = pl.BlockSpec(memory_space=pltpu.VMEM)
SMEM = pl.BlockSpec(memory_space=pltpu.SMEM)
HBM = pl.BlockSpec(memory_space=pltpu.HBM)
DMA = pltpu.SemaphoreType.DMA


def hot(ids, rows):
    row = lax.broadcasted_iota(jnp.int32, (rows, ids.shape[1]), 0)
    return jnp.where(row == ids, 1.0, 0.0).astype(BF)


def pair_ids(ids_ref, pair):
    return jnp.concatenate([ids_ref[pl.ds(2 * pair, 1), :], ids_ref[pl.ds(2 * pair + 1, 1), :]], axis=1)


def pick_lane(block, lane):
    lanes = lax.broadcasted_iota(jnp.int32, block.shape, 1)
    return jnp.sum(jnp.where(lanes == lane, block, 0.0), axis=1, keepdims=True)


def dot_nn(a, b):
    return lax.dot_general(a, b, (((1,), (0,)), ((), ())), preferred_element_type=F32)


def dot_nt(a, b):
    return lax.dot_general(a, b, (((1,), (1,)), ((), ())), preferred_element_type=F32)


def dot_tn(a, b):
    return lax.dot_general(a, b, (((0,), (0,)), ((), ())), preferred_element_type=F32)


def weight_kernel(count, rel_ids, rel, weights, table, last, sems):
    live = count[0, 0]
    whole = rel.shape[1] // LANES * LANES
    loads = [pltpu.make_async_copy(rel.at[:, pl.ds(0, whole)], table.at[:, pl.ds(0, whole)], sems.at[0])]
    if whole < rel.shape[1]:
        loads.append(pltpu.make_async_copy(rel.at[:, pl.ds(whole, rel.shape[1] - whole)], last, sems.at[1]))
    for load in loads:
        load.start()
    weights[...] = jnp.zeros_like(weights)
    for load in loads:
        load.wait()
    if whole < rel.shape[1]:
        table[:, whole : rel.shape[1]] = last[...]

    @pl.loop(0, (live + 1) // 2)
    def _(pair):
        total = weights[...]
        lanes = lax.broadcasted_iota(jnp.int32, weights.shape, 1)
        for k in range(2):
            tile = 2 * pair + k
            rid = rel_ids[tile]
            at = rid // LANES * LANES
            w = pick_lane(table[:, pl.ds(pl.multiple_of(at, LANES), LANES)], rid - at)
            total = jnp.where(lanes == tile, jnp.where(tile < live, w, 0.0), total)
        weights[...] = total


def query_kernel(count, ent, heads, weights, query, out, sems):
    live = count[0, 0]
    pairs = 2 * ((live + 3) // 4)
    half, edges = ent.shape[0] // 2, heads.shape[1]

    def put(pair):
        return pltpu.make_async_copy(out.at[pair], query.at[pl.ds(2 * pair, 2)], sems.at[pair])

    @pl.loop(0, pairs)
    def _(pair):
        head = dot_nn(ent[...], hot(pair_ids(heads, pair), ent.shape[1]))
        for k in range(2):
            w = pick_lane(weights[...], 2 * pair + k)
            hr = head[:half, k * edges : (k + 1) * edges]
            hi = head[half:, k * edges : (k + 1) * edges]
            wr, wi = w[:half], w[half:]
            out[pair, k] = jnp.concatenate([hr * wr - hi * wi, hr * wi + hi * wr], axis=0).astype(BF)
        put(pair).start()

    @pl.loop(0, pairs)
    def _(pair):
        put(pair).wait()


def tail_kernel(count, query, partner, hub, tails, pick, diff, grads, table, acc, qin, picks, diffs, moves, qsem, psem, dsem):
    dim, rows = hub.shape[0], partner.shape[1]
    edges = tails.shape[1]
    live = count[0, 0]
    quads = (live + 3) // 4
    pairs = 2 * quads

    def fetch(pair):
        both = pl.ds(2 * pair, 2)
        return pltpu.make_async_copy(query.at[both], qin.at[both], qsem.at[pair])

    def put_pick(pair, slot):
        return pltpu.make_async_copy(picks.at[slot], pick.at[pair], psem.at[slot])

    def put_diff(pair):
        both = pl.ds(2 * pair, 2)
        return pltpu.make_async_copy(diffs.at[both], diff.at[both], dsem.at[pair])

    @pl.loop(0, pairs)
    def _(pair):
        fetch(pair).start()

    table[:, :rows] = partner[:dim]
    table[:, rows:] = hub[...]
    acc[...] = jnp.zeros_like(acc)
    moves[...] = jnp.zeros_like(moves)
    eye = lax.broadcasted_iota(jnp.int32, (edges, edges), 0) == lax.broadcasted_iota(
        jnp.int32, (edges, edges), 1
    )

    def pick_tails(pair, slot):
        picks[slot] = dot_nn(table[...], hot(pair_ids(tails, pair), table.shape[1])).astype(BF)

    def spread(pair, slot):
        acc[...] += dot_nt(moves[slot], hot(pair_ids(tails, pair), table.shape[1]))

    pick_tails(0, 0)
    put_pick(0, 0).start()

    @pl.loop(0, quads)
    def _(quad):
        for slot in range(2):
            pair = 2 * quad + slot
            fetch(pair).wait()

            @pl.when(pair >= 1)
            def _():
                put_pick(pair - 1, 1 - slot).wait()

            ats = [slice(k * edges, (k + 1) * edges) for k in range(2)]
            qs = [qin[2 * pair + k] for k in range(2)]
            scores = [dot_tn(picks[slot, :, ats[k]], qs[k]) for k in range(2)]
            spread(jnp.maximum(pair - 1, 0), 1 - slot)
            ds = []
            for k in range(2):
                tile = 2 * pair + k
                top = jnp.max(scores[k], axis=0, keepdims=True)
                expo = jnp.exp(scores[k] - top)
                probs = expo * (1.0 / jnp.sum(expo, axis=0, keepdims=True))
                d = jnp.where(eye, probs - 1.0, probs)
                if slot + k:
                    d = jnp.where(tile < live, d, 0.0)
                ds.append(d.astype(BF))
                diffs[tile] = ds[k]
            pick_tails(jnp.minimum(pair + 1, pairs - 1), 1 - slot)
            for k in range(2):
                moves[slot, :, ats[k]] = dot_nt(qs[k], ds[k]).astype(BF)
            put_diff(pair).start()

            @pl.when(pair + 1 < pairs)
            def _():
                put_pick(pair + 1, 1 - slot).start()

    spread(pairs - 1, 1)
    chunks, step = grads.shape[0], grads.shape[1]
    for c in range(chunks):
        n = min(step, dim - c * step)
        grads[c, :n] = acc[c * step : c * step + n].astype(BF)
        if n < step:
            grads[c, n:] = jnp.zeros((step - n, grads.shape[2]), BF)
    put_pick(pairs - 1, 1).wait()

    @pl.loop(0, pairs)
    def _(pair):
        put_diff(pair).wait()


def head_kernel(count, pick, diff, weights, heads, ent, base, pin, din, moves, acc, psem, dsem, sem):
    half = acc.shape[0] // 2
    edges = heads.shape[1]
    live = count[0, 0]
    quads = (live + 3) // 4
    pairs = 2 * quads

    def get_pick(pair):
        return pltpu.make_async_copy(pick.at[pair], pin.at[pair], psem.at[pair])

    def get_diff(pair):
        both = pl.ds(2 * pair, 2)
        return pltpu.make_async_copy(diff.at[both], din.at[both], dsem.at[pair])

    @pl.loop(0, pairs)
    def _(pair):
        get_pick(pair).start()
        get_diff(pair).start()

    acc[...] = jnp.zeros_like(acc)
    moves[...] = jnp.zeros_like(moves)

    def spread(pair, slot):
        acc[...] += dot_nt(moves[slot], hot(pair_ids(heads, pair), acc.shape[1]))

    @pl.loop(0, quads)
    def _(quad):
        for slot in range(2):
            pair = 2 * quad + slot
            get_pick(pair).wait()
            get_diff(pair).wait()
            ats = [slice(k * edges, (k + 1) * edges) for k in range(2)]
            d_query = [dot_nn(pin[pair, :, ats[k]], din[2 * pair + k]) for k in range(2)]
            spread(jnp.maximum(pair - 1, 0), 1 - slot)
            for k in range(2):
                w = pick_lane(weights[...], 2 * pair + k)
                dr, di = d_query[k][:half], d_query[k][half:]
                wr, wi = w[:half], w[half:]
                moves[slot, :, ats[k]] = jnp.concatenate(
                    [dr * wr + di * wi, di * wr - dr * wi], axis=0
                ).astype(BF)

    spread(pairs - 1, 1)
    acc[...] = ent[...].astype(F32) - learn_rate * acc[...]
    put = pltpu.make_async_copy(acc, base.at[0], sem)
    put.start()
    put.wait()


def parts_of(dim, step):
    return [(at, min(step, dim - at)) for at in range(0, dim, step)]


def reorder_kernel(matching, rows, out, sems):
    puts = [
        pltpu.make_async_copy(rows.at[matching[g]], out.at[g], sems.at[g]) for g in range(out.shape[0])
    ]
    for put in puts:
        put.start()
    for put in puts:
        put.wait()


def return_kernel(matching, back, hub, base, out, held, sem):
    load = pltpu.make_async_copy(base.at[0], held, sem)
    load.start()
    rows = out.shape[2] - hub.shape[2]
    total = hub[0].astype(F32)
    for m in range(1, hub.shape[0]):
        total += hub[m].astype(F32)
    total = total.astype(BF)
    for g in range(out.shape[0]):
        out[matching[g], :, :rows] = back[g, :, :rows]
        out[g, :, rows:] = total
    load.wait()


def update_kernel(base, hub, last, new_ent, new_hub):
    dim, rows = base.shape
    for i, (at, n) in enumerate(parts_of(dim, last.shape[1])):
        rng = slice(at, at + n)
        got = last[i, :n].astype(F32)
        new_ent[rng] = (base[rng] - learn_rate * got[:, :rows]).astype(BF)
        new_hub[rng] = (hub[rng].astype(F32) - learn_rate * got[:, rows:]).astype(BF)


def call(kernel, out_shape, in_specs, out_specs, flops, moved, scratch=(), exps=0, vmem=32, aliases={}):
    return pl.pallas_call(
        kernel,
        out_shape=out_shape,
        in_specs=in_specs,
        out_specs=out_specs,
        scratch_shapes=scratch,
        input_output_aliases=aliases,
        compiler_params=pltpu.CompilerParams(vmem_limit_bytes=vmem * 1024 * 1024),
        cost_estimate=pl.CostEstimate(flops=flops, bytes_accessed=moved, transcendentals=exps),
    )


shape = jax.ShapeDtypeStruct


def run_weights(tile_count, tile_rel, rel):
    dim, rels = rel.shape
    rest = rels % LANES or LANES
    return call(
        weight_kernel,
        shape((dim, LANES), F32),
        [SMEM, SMEM, HBM],
        VMEM,
        40 * dim * dim * dim,
        4 * rel.size,
        [pltpu.VMEM((dim, -(-rels // LANES) * LANES), F32), pltpu.VMEM((dim, rest), F32), DMA((2,))],
        vmem=60,
    )(tile_count, tile_rel, rel)


def run_query(tile_count, ent, head_index, weights):
    dim, rows = ent.shape
    tiles, edges = head_index.shape
    return call(
        query_kernel,
        shape((2 * tiles, dim, edges), BF),
        [SMEM, VMEM, VMEM, VMEM],
        HBM,
        2 * tiles * edges * dim * rows,
        2 * tiles * dim * edges,
        [pltpu.VMEM((tiles // 2, 2, dim, edges), BF), DMA((tiles // 2,))],
        vmem=60,
    )(tile_count, ent, head_index, weights)


def run_tail(tile_count, query, partner, hub, tail_index, groups, step):
    tiles, edges = tail_index.shape
    dim = query.shape[1]
    rows, hubs = partner.shape[1], hub.shape[1]
    return call(
        tail_kernel,
        [
            shape((tiles, dim, 2 * edges), BF),
            shape((3 * tiles, edges, edges), BF),
            shape((groups, step, rows + hubs), BF),
        ],
        [SMEM, HBM, VMEM, VMEM, VMEM],
        [HBM, HBM, VMEM],
        4 * tiles * edges * dim * (rows + hubs + edges),
        8 * tiles * dim * edges,
        [
            pltpu.VMEM((dim, rows + hubs), BF),
            pltpu.VMEM((dim, rows + hubs), F32),
            pltpu.VMEM((tiles, dim, edges), BF),
            pltpu.VMEM((2, dim, 2 * edges), BF),
            pltpu.VMEM((tiles, edges, edges), BF),
            pltpu.VMEM((2, dim, 2 * edges), BF),
            DMA((tiles // 2,)),
            DMA((2,)),
            DMA((tiles // 2,)),
        ],
        tiles * edges * edges,
        vmem=50,
    )(tile_count, query, partner, hub, tail_index)


def run_head(tile_count, pick, diff, weights, head_index, ent):
    tiles, edges = head_index.shape
    dim, rows = ent.shape
    return call(
        head_kernel,
        shape((8, dim, rows), F32),
        [SMEM, HBM, HBM, VMEM, VMEM, VMEM],
        HBM,
        2 * tiles * edges * dim * (rows + edges),
        6 * tiles * dim * edges,
        [
            pltpu.VMEM((tiles // 2, dim, 2 * edges), BF),
            pltpu.VMEM((tiles, edges, edges), BF),
            pltpu.VMEM((2, dim, 2 * edges), BF),
            pltpu.VMEM((dim, rows), F32),
            DMA((tiles // 2,)),
            DMA((tiles // 2,)),
            DMA(()),
        ],
        vmem=60,
    )(tile_count, pick, diff, weights, head_index, ent)


def make(groups, members):
    def shards(entities, hub_rows, relations, matching, head_index, tail_index, tile_rel, tile_count):
        ent, hub, rel = entities.T, hub_rows.T, relations.T
        dim, rows = ent.shape
        hubs = hub.shape[1]
        step = -(-dim // (8 * groups)) * 8

        high, wide = dim // 8, rows // LANES
        cut = ent.reshape(high, 8, wide, LANES).transpose(0, 2, 1, 3)
        cut = lax.all_to_all(cut.reshape(groups, -1, 8, LANES), "group", 0, 0)
        weights = run_weights(tile_count, tile_rel, rel)
        cut, weights = lax.optimization_barrier((cut, weights))
        cut = call(
            reorder_kernel, shape(cut.shape, BF), [SMEM, VMEM], HBM, 0, 4 * cut.size, [DMA((groups,))]
        )(matching, cut)
        partner = lax.all_to_all(cut, "group", 0, 0).reshape(high, wide, 8, LANES)
        partner = partner.transpose(0, 2, 1, 3).reshape(dim, rows)
        query = run_query(tile_count, ent, head_index, weights)
        pick, diff, grads = run_tail(tile_count, query, partner, hub, tail_index, groups, step)

        got = lax.all_to_all(grads, "group", 0, 0)
        got, pick, diff = lax.optimization_barrier((got, pick, diff))
        part = jnp.sum(got[:, :, rows:].astype(F32), axis=0).astype(BF)
        other = lax.ppermute(part, "member", [(m, m ^ 1) for m in range(members)])
        part = (part.astype(F32) + other.astype(F32)).astype(BF)
        cores = [list(range(core, members, 2)) for core in range(2)]
        parts = jnp.broadcast_to(part[None], (members // 2,) + part.shape)
        parts = lax.all_to_all(parts, "member", 0, 0, axis_index_groups=cores)
        base = run_head(tile_count, pick, diff, weights, head_index, ent)
        parts, base = lax.optimization_barrier((parts, base))
        sent, base = call(
            return_kernel,
            [shape(got.shape, BF), shape((dim, rows), F32)],
            [SMEM, VMEM, VMEM, HBM],
            [VMEM, VMEM],
            0,
            4 * got.size,
            [DMA(())],
            vmem=54,
        )(matching, got, parts, base)
        last = lax.all_to_all(sent, "group", 0, 0)
        new_ent, new_hub = call(
            update_kernel,
            [shape((dim, rows), BF), shape((dim, hubs), BF)],
            [VMEM, VMEM, VMEM],
            [VMEM, VMEM],
            0,
            8 * dim * rows,
        )(base, hub, last)
        return (new_ent.T, new_hub.T)

    return shards


def solution(mesh):
    placed = (
        P(("group", "member"), None),
        P(),
        P(),
        P(),
        P(("group", "member"), None),
        P(("group", "member"), None),
        P(("group", "member")),
        P("group", "member"),
    )
    return jax.shard_map(
        make(mesh.shape["group"], mesh.shape["member"]),
        mesh=mesh,
        in_specs=placed,
        out_specs=(P(("group", "member"), None), P()),
        check_vma=False,
    )
```

```python
import jax
import jax.numpy as jnp
from jax import lax
from jax.experimental import pallas as pl
from jax.experimental.pallas import tpu as pltpu
from jax.sharding import PartitionSpec as P

learn_rate = 0.1
BF = jnp.bfloat16
F32 = jnp.float32
LANES = 128
VMEM = pl.BlockSpec(memory_space=pltpu.VMEM)
SMEM = pl.BlockSpec(memory_space=pltpu.SMEM)
HBM = pl.BlockSpec(memory_space=pltpu.HBM)
DMA = pltpu.SemaphoreType.DMA


def hot(ids, rows):
    row = lax.broadcasted_iota(jnp.int32, (rows, ids.shape[1]), 0)
    return jnp.where(row == ids, 1.0, 0.0).astype(BF)


def pair_ids(ids_ref, pair):
    return jnp.concatenate([ids_ref[pl.ds(2 * pair, 1), :], ids_ref[pl.ds(2 * pair + 1, 1), :]], axis=1)


def pick_lane(block, lane):
    lanes = lax.broadcasted_iota(jnp.int32, block.shape, 1)
    return jnp.sum(jnp.where(lanes == lane, block, 0.0), axis=1, keepdims=True)


def dot_nn(a, b):
    return lax.dot_general(a, b, (((1,), (0,)), ((), ())), preferred_element_type=F32)


def dot_nt(a, b):
    return lax.dot_general(a, b, (((1,), (1,)), ((), ())), preferred_element_type=F32)


def dot_tn(a, b):
    return lax.dot_general(a, b, (((0,), (0,)), ((), ())), preferred_element_type=F32)


def weight_kernel(count, rel_ids, rel, weights, table, last, sems):
    live = count[0, 0]
    whole = rel.shape[1] // LANES * LANES
    loads = [pltpu.make_async_copy(rel.at[:, pl.ds(0, whole)], table.at[:, pl.ds(0, whole)], sems.at[0])]
    if whole < rel.shape[1]:
        loads.append(pltpu.make_async_copy(rel.at[:, pl.ds(whole, rel.shape[1] - whole)], last, sems.at[1]))
    for load in loads:
        load.start()
    weights[...] = jnp.zeros_like(weights)
    for load in loads:
        load.wait()
    if whole < rel.shape[1]:
        table[:, whole : rel.shape[1]] = last[...]

    @pl.loop(0, (live + 1) // 2)
    def _(pair):
        total = weights[...]
        lanes = lax.broadcasted_iota(jnp.int32, weights.shape, 1)
        for k in range(2):
            tile = 2 * pair + k
            rid = rel_ids[tile]
            at = rid // LANES * LANES
            w = pick_lane(table[:, pl.ds(pl.multiple_of(at, LANES), LANES)], rid - at)
            total = jnp.where(lanes == tile, jnp.where(tile < live, w, 0.0), total)
        weights[...] = total


def query_kernel(count, ent, heads, weights, query, out, sems):
    live = count[0, 0]
    pairs = 2 * ((live + 3) // 4)
    half, edges = ent.shape[0] // 2, heads.shape[1]

    def put(pair):
        return pltpu.make_async_copy(out.at[pair], query.at[pl.ds(2 * pair, 2)], sems.at[pair])

    @pl.loop(0, pairs)
    def _(pair):
        head = dot_nn(ent[...], hot(pair_ids(heads, pair), ent.shape[1]))
        for k in range(2):
            w = pick_lane(weights[...], 2 * pair + k)
            hr = head[:half, k * edges : (k + 1) * edges]
            hi = head[half:, k * edges : (k + 1) * edges]
            wr, wi = w[:half], w[half:]
            out[pair, k] = jnp.concatenate([hr * wr - hi * wi, hr * wi + hi * wr], axis=0).astype(BF)
        put(pair).start()

    @pl.loop(0, pairs)
    def _(pair):
        put(pair).wait()


def tail_kernel(count, query, partner, hub, tails, pick, diff, grads, table, acc, qin, picks, diffs, moves, qsem, psem, dsem):
    dim, rows = hub.shape[0], partner.shape[1]
    edges = tails.shape[1]
    live = count[0, 0]
    quads = (live + 3) // 4
    pairs = 2 * quads

    def fetch(pair):
        both = pl.ds(2 * pair, 2)
        return pltpu.make_async_copy(query.at[both], qin.at[both], qsem.at[pair])

    def put_pick(pair, slot):
        return pltpu.make_async_copy(picks.at[slot], pick.at[pair], psem.at[slot])

    def put_diff(pair):
        both = pl.ds(2 * pair, 2)
        return pltpu.make_async_copy(diffs.at[both], diff.at[both], dsem.at[pair])

    @pl.loop(0, pairs)
    def _(pair):
        fetch(pair).start()

    table[:, :rows] = partner[:dim]
    table[:, rows:] = hub[...]
    acc[...] = jnp.zeros_like(acc)
    moves[...] = jnp.zeros_like(moves)
    eye = lax.broadcasted_iota(jnp.int32, (edges, edges), 0) == lax.broadcasted_iota(
        jnp.int32, (edges, edges), 1
    )

    def pick_tails(pair, slot):
        picks[slot] = dot_nn(table[...], hot(pair_ids(tails, pair), table.shape[1])).astype(BF)

    def spread(pair, slot):
        acc[...] += dot_nt(moves[slot], hot(pair_ids(tails, pair), table.shape[1]))

    pick_tails(0, 0)
    put_pick(0, 0).start()

    @pl.loop(0, quads)
    def _(quad):
        for slot in range(2):
            pair = 2 * quad + slot
            fetch(pair).wait()

            @pl.when(pair >= 1)
            def _():
                put_pick(pair - 1, 1 - slot).wait()

            ats = [slice(k * edges, (k + 1) * edges) for k in range(2)]
            qs = [qin[2 * pair + k] for k in range(2)]
            scores = [dot_tn(picks[slot, :, ats[k]], qs[k]) for k in range(2)]
            spread(jnp.maximum(pair - 1, 0), 1 - slot)
            ds = []
            for k in range(2):
                tile = 2 * pair + k
                top = jnp.max(scores[k], axis=0, keepdims=True)
                expo = jnp.exp(scores[k] - top)
                probs = expo * (1.0 / jnp.sum(expo, axis=0, keepdims=True))
                d = jnp.where(eye, probs - 1.0, probs)
                if slot + k:
                    d = jnp.where(tile < live, d, 0.0)
                ds.append(d.astype(BF))
                diffs[tile] = ds[k]
            pick_tails(jnp.minimum(pair + 1, pairs - 1), 1 - slot)
            for k in range(2):
                moves[slot, :, ats[k]] = dot_nt(qs[k], ds[k]).astype(BF)
            put_diff(pair).start()

            @pl.when(pair + 1 < pairs)
            def _():
                put_pick(pair + 1, 1 - slot).start()

    spread(pairs - 1, 1)
    chunks, step = grads.shape[0], grads.shape[1]
    for c in range(chunks):
        n = min(step, dim - c * step)
        grads[c, :n] = acc[c * step : c * step + n].astype(BF)
        if n < step:
            grads[c, n:] = jnp.zeros((step - n, grads.shape[2]), BF)
    put_pick(pairs - 1, 1).wait()

    @pl.loop(0, pairs)
    def _(pair):
        put_diff(pair).wait()


def head_kernel(count, pick, diff, weights, heads, ent, base, pin, din, moves, acc, psem, dsem, sem):
    half = acc.shape[0] // 2
    edges = heads.shape[1]
    live = count[0, 0]
    quads = (live + 3) // 4
    pairs = 2 * quads

    def get_pick(pair):
        return pltpu.make_async_copy(pick.at[pair], pin.at[pair], psem.at[pair])

    def get_diff(pair):
        both = pl.ds(2 * pair, 2)
        return pltpu.make_async_copy(diff.at[both], din.at[both], dsem.at[pair])

    @pl.loop(0, pairs)
    def _(pair):
        get_pick(pair).start()
        get_diff(pair).start()

    acc[...] = jnp.zeros_like(acc)
    moves[...] = jnp.zeros_like(moves)

    def spread(pair, slot):
        acc[...] += dot_nt(moves[slot], hot(pair_ids(heads, pair), acc.shape[1]))

    @pl.loop(0, quads)
    def _(quad):
        for slot in range(2):
            pair = 2 * quad + slot
            get_pick(pair).wait()
            get_diff(pair).wait()
            ats = [slice(k * edges, (k + 1) * edges) for k in range(2)]
            d_query = [dot_nn(pin[pair, :, ats[k]], din[2 * pair + k]) for k in range(2)]
            spread(jnp.maximum(pair - 1, 0), 1 - slot)
            for k in range(2):
                w = pick_lane(weights[...], 2 * pair + k)
                dr, di = d_query[k][:half], d_query[k][half:]
                wr, wi = w[:half], w[half:]
                moves[slot, :, ats[k]] = jnp.concatenate(
                    [dr * wr + di * wi, di * wr - dr * wi], axis=0
                ).astype(BF)

    spread(pairs - 1, 1)
    acc[...] = ent[...].astype(F32) - learn_rate * acc[...]
    put = pltpu.make_async_copy(acc, base.at[0], sem)
    put.start()
    put.wait()


def parts_of(dim, step):
    return [(at, min(step, dim - at)) for at in range(0, dim, step)]


def reorder_kernel(matching, rows, out, sems):
    puts = [
        pltpu.make_async_copy(rows.at[matching[g]], out.at[g], sems.at[g]) for g in range(out.shape[0])
    ]
    for put in puts:
        put.start()
    for put in puts:
        put.wait()


def return_kernel(matching, back, hub, base, out, held, sem):
    load = pltpu.make_async_copy(base.at[0], held, sem)
    load.start()
    rows = out.shape[2] - hub.shape[2]
    total = hub[0].astype(F32)
    for m in range(1, hub.shape[0]):
        total += hub[m].astype(F32)
    total = total.astype(BF)
    for g in range(out.shape[0]):
        out[matching[g], :, :rows] = back[g, :, :rows]
        out[g, :, rows:] = total
    load.wait()


def update_kernel(base, hub, last, new_ent, new_hub):
    dim, rows = base.shape
    for i, (at, n) in enumerate(parts_of(dim, last.shape[1])):
        rng = slice(at, at + n)
        got = last[i, :n].astype(F32)
        new_ent[rng] = (base[rng] - learn_rate * got[:, :rows]).astype(BF)
        new_hub[rng] = (hub[rng].astype(F32) - learn_rate * got[:, rows:]).astype(BF)


def call(kernel, out_shape, in_specs, out_specs, flops, moved, scratch=(), exps=0, vmem=32, aliases={}):
    return pl.pallas_call(
        kernel,
        out_shape=out_shape,
        in_specs=in_specs,
        out_specs=out_specs,
        scratch_shapes=scratch,
        input_output_aliases=aliases,
        compiler_params=pltpu.CompilerParams(vmem_limit_bytes=vmem * 1024 * 1024),
        cost_estimate=pl.CostEstimate(flops=flops, bytes_accessed=moved, transcendentals=exps),
    )


shape = jax.ShapeDtypeStruct


def run_weights(tile_count, tile_rel, rel):
    dim, rels = rel.shape
    rest = rels % LANES or LANES
    return call(
        weight_kernel,
        shape((dim, LANES), F32),
        [SMEM, SMEM, HBM],
        VMEM,
        40 * dim * dim * dim,
        4 * rel.size,
        [pltpu.VMEM((dim, -(-rels // LANES) * LANES), F32), pltpu.VMEM((dim, rest), F32), DMA((2,))],
        vmem=60,
    )(tile_count, tile_rel, rel)


def run_query(tile_count, ent, head_index, weights):
    dim, rows = ent.shape
    tiles, edges = head_index.shape
    return call(
        query_kernel,
        shape((2 * tiles, dim, edges), BF),
        [SMEM, VMEM, VMEM, VMEM],
        HBM,
        2 * tiles * edges * dim * rows,
        2 * tiles * dim * edges,
        [pltpu.VMEM((tiles // 2, 2, dim, edges), BF), DMA((tiles // 2,))],
        vmem=60,
    )(tile_count, ent, head_index, weights)


def run_tail(tile_count, query, partner, hub, tail_index, groups, step):
    tiles, edges = tail_index.shape
    dim = query.shape[1]
    rows, hubs = partner.shape[1], hub.shape[1]
    return call(
        tail_kernel,
        [
            shape((tiles, dim, 2 * edges), BF),
            shape((3 * tiles, edges, edges), BF),
            shape((groups, step, rows + hubs), BF),
        ],
        [SMEM, HBM, VMEM, VMEM, VMEM],
        [HBM, HBM, VMEM],
        4 * tiles * edges * dim * (rows + hubs + edges),
        8 * tiles * dim * edges,
        [
            pltpu.VMEM((dim, rows + hubs), BF),
            pltpu.VMEM((dim, rows + hubs), F32),
            pltpu.VMEM((tiles, dim, edges), BF),
            pltpu.VMEM((2, dim, 2 * edges), BF),
            pltpu.VMEM((tiles, edges, edges), BF),
            pltpu.VMEM((2, dim, 2 * edges), BF),
            DMA((tiles // 2,)),
            DMA((2,)),
            DMA((tiles // 2,)),
        ],
        tiles * edges * edges,
        vmem=50,
    )(tile_count, query, partner, hub, tail_index)


def run_head(tile_count, pick, diff, weights, head_index, ent):
    tiles, edges = head_index.shape
    dim, rows = ent.shape
    return call(
        head_kernel,
        shape((8, dim, rows), F32),
        [SMEM, HBM, HBM, VMEM, VMEM, VMEM],
        HBM,
        2 * tiles * edges * dim * (rows + edges),
        6 * tiles * dim * edges,
        [
            pltpu.VMEM((tiles // 2, dim, 2 * edges), BF),
            pltpu.VMEM((tiles, edges, edges), BF),
            pltpu.VMEM((2, dim, 2 * edges), BF),
            pltpu.VMEM((dim, rows), F32),
            DMA((tiles // 2,)),
            DMA((tiles // 2,)),
            DMA(()),
        ],
        vmem=60,
    )(tile_count, pick, diff, weights, head_index, ent)


def make(groups, members):
    def shards(entities, hub_rows, relations, matching, head_index, tail_index, tile_rel, tile_count):
        ent, hub, rel = entities.T, hub_rows.T, relations.T
        dim, rows = ent.shape
        hubs = hub.shape[1]
        step = -(-dim // (8 * groups)) * 8

        high, wide = dim // 8, rows // LANES
        cut = ent.reshape(high, 8, wide, LANES).transpose(0, 2, 1, 3)
        cut = lax.all_to_all(cut.reshape(groups, -1, 8, LANES), "group", 0, 0)
        weights = run_weights(tile_count, tile_rel, rel)
        cut, weights = lax.optimization_barrier((cut, weights))
        cut = call(
            reorder_kernel, shape(cut.shape, BF), [SMEM, VMEM], HBM, 0, 4 * cut.size, [DMA((groups,))]
        )(matching, cut)
        partner = lax.all_to_all(cut, "group", 0, 0).reshape(high, wide, 8, LANES)
        partner = partner.transpose(0, 2, 1, 3).reshape(dim, rows)
        query = run_query(tile_count, ent, head_index, weights)
        pick, diff, grads = run_tail(tile_count, query, partner, hub, tail_index, groups, step)

        got = lax.all_to_all(grads, "group", 0, 0)
        got, pick, diff = lax.optimization_barrier((got, pick, diff))
        part = jnp.sum(got[:, :, rows:].astype(F32), axis=0).astype(BF)
        other = lax.ppermute(part, "member", [(m, m ^ 1) for m in range(members)])
        part = (part.astype(F32) + other.astype(F32)).astype(BF)
        cores = [list(range(core, members, 2)) for core in range(2)]
        parts = jnp.broadcast_to(part[None], (members // 2,) + part.shape)
        parts = lax.all_to_all(parts, "member", 0, 0, axis_index_groups=cores)
        base = run_head(tile_count, pick, diff, weights, head_index, ent)
        parts, base = lax.optimization_barrier((parts, base))
        sent, base = call(
            return_kernel,
            [shape(got.shape, BF), shape((dim, rows), F32)],
            [SMEM, VMEM, VMEM, HBM],
            [VMEM, VMEM],
            0,
            4 * got.size,
            [DMA(())],
            vmem=50,
        )(matching, got, parts, base)
        last = lax.all_to_all(sent, "group", 0, 0)
        new_ent, new_hub = call(
            update_kernel,
            [shape((dim, rows), BF), shape((dim, hubs), BF)],
            [VMEM, VMEM, VMEM],
            [VMEM, VMEM],
            0,
            8 * dim * rows,
        )(base, hub, last)
        return (new_ent.T, new_hub.T)

    return shards


def solution(mesh):
    placed = (
        P(("group", "member"), None),
        P(),
        P(),
        P(),
        P(("group", "member"), None),
        P(("group", "member"), None),
        P(("group", "member")),
        P("group", "member"),
    )
    return jax.shard_map(
        make(mesh.shape["group"], mesh.shape["member"]),
        mesh=mesh,
        in_specs=placed,
        out_specs=(P(("group", "member"), None), P()),
        check_vma=False,
    )
```

```python
import jax
import jax.numpy as jnp
from jax import lax
from jax.experimental import pallas as pl
from jax.experimental.pallas import tpu as pltpu
from jax.sharding import PartitionSpec as P

learn_rate = 0.1
BF = jnp.bfloat16
F32 = jnp.float32
LANES = 128
VMEM = pl.BlockSpec(memory_space=pltpu.VMEM)
SMEM = pl.BlockSpec(memory_space=pltpu.SMEM)
HBM = pl.BlockSpec(memory_space=pltpu.HBM)
DMA = pltpu.SemaphoreType.DMA


def hot(ids, rows):
    row = lax.broadcasted_iota(jnp.int32, (rows, ids.shape[1]), 0).astype(jnp.int16)
    return jnp.where(row == ids.astype(jnp.int16), jnp.ones((), BF), jnp.zeros((), BF))


def pair_ids(ids_ref, pair):
    return jnp.concatenate([ids_ref[pl.ds(2 * pair, 1), :], ids_ref[pl.ds(2 * pair + 1, 1), :]], axis=1)


def pick_lane(block, lane):
    lanes = lax.broadcasted_iota(jnp.int32, block.shape, 1)
    return jnp.sum(jnp.where(lanes == lane, block, 0.0), axis=1, keepdims=True)


def dot_nn(a, b):
    return lax.dot_general(a, b, (((1,), (0,)), ((), ())), preferred_element_type=F32)


def dot_nt(a, b):
    return lax.dot_general(a, b, (((1,), (1,)), ((), ())), preferred_element_type=F32)


def dot_tn(a, b):
    return lax.dot_general(a, b, (((0,), (0,)), ((), ())), preferred_element_type=F32)


def weight_kernel(count, rel_ids, rel, weights, table, last, sems):
    live = count[0, 0]
    whole = rel.shape[1] // LANES * LANES
    loads = [pltpu.make_async_copy(rel.at[:, pl.ds(0, whole)], table.at[:, pl.ds(0, whole)], sems.at[0])]
    if whole < rel.shape[1]:
        loads.append(pltpu.make_async_copy(rel.at[:, pl.ds(whole, rel.shape[1] - whole)], last, sems.at[1]))
    for load in loads:
        load.start()
    weights[...] = jnp.zeros_like(weights)
    for load in loads:
        load.wait()
    if whole < rel.shape[1]:
        table[:, whole : rel.shape[1]] = last[...]

    @pl.loop(0, (live + 1) // 2)
    def _(pair):
        total = weights[...]
        lanes = lax.broadcasted_iota(jnp.int32, weights.shape, 1)
        for k in range(2):
            tile = 2 * pair + k
            rid = rel_ids[tile]
            at = rid // LANES * LANES
            w = pick_lane(table[:, pl.ds(pl.multiple_of(at, LANES), LANES)], rid - at)
            total = jnp.where(lanes == tile, jnp.where(tile < live, w, 0.0), total)
        weights[...] = total


def query_kernel(count, ent, heads, weights, query, out, sems):
    live = count[0, 0]
    pairs = 2 * ((live + 3) // 4)
    half, edges = ent.shape[0] // 2, heads.shape[1]

    def put(pair):
        return pltpu.make_async_copy(out.at[pair], query.at[pl.ds(2 * pair, 2)], sems.at[pair])

    @pl.loop(0, pairs)
    def _(pair):
        head = dot_nn(ent[...], hot(pair_ids(heads, pair), ent.shape[1]))
        for k in range(2):
            w = pick_lane(weights[...], 2 * pair + k)
            hr = head[:half, k * edges : (k + 1) * edges]
            hi = head[half:, k * edges : (k + 1) * edges]
            wr, wi = w[:half], w[half:]
            out[pair, k] = jnp.concatenate([hr * wr - hi * wi, hr * wi + hi * wr], axis=0).astype(BF)
        put(pair).start()

    @pl.loop(0, pairs)
    def _(pair):
        put(pair).wait()


def sizes(dim, rows, hubs, chunks):
    return dim // 8 * (rows // LANES) // chunks, -(-(dim // 8 * (hubs // LANES)) // chunks)


def places(dim, rows, hubs, chunks):
    own, more = sizes(dim, rows, hubs, chunks)
    found = []
    for first, base, width, each in ((0, 0, rows, own), (own, rows, hubs, more)):
        wide = width // LANES
        for t in range(dim // 8 * wide):
            found.append((t // each, first + t % each, t // wide * 8, base + t % wide * LANES))
    return found


def tail_kernel(count, query, partner, hub, tails, pick, diff, grads, table, acc, qin, picks, diffs, moves, qsem, psem, dsem):
    dim, rows = hub.shape[0], partner.shape[1]
    edges = tails.shape[1]
    live = count[0, 0]
    quads = (live + 3) // 4
    pairs = 2 * quads

    def fetch(pair):
        both = pl.ds(2 * pair, 2)
        return pltpu.make_async_copy(query.at[both], qin.at[both], qsem.at[pair])

    def put_pick(pair, slot):
        return pltpu.make_async_copy(picks.at[slot], pick.at[pair], psem.at[slot])

    def put_diff(pair):
        both = pl.ds(2 * pair, 2)
        return pltpu.make_async_copy(diffs.at[both], diff.at[both], dsem.at[pair])

    @pl.loop(0, pairs)
    def _(pair):
        fetch(pair).start()

    table[:, :rows] = partner[:dim]
    table[:, rows:] = hub[...]
    acc[...] = jnp.zeros_like(acc)
    moves[...] = jnp.zeros_like(moves)
    eye = lax.broadcasted_iota(jnp.int32, (edges, edges), 0) == lax.broadcasted_iota(
        jnp.int32, (edges, edges), 1
    )

    def pick_tails(pair, slot):
        picks[slot] = dot_nn(table[...], hot(pair_ids(tails, pair), table.shape[1])).astype(BF)

    def spread(pair, slot):
        acc[...] += dot_nt(moves[slot], hot(pair_ids(tails, pair), table.shape[1]))

    pick_tails(0, 0)
    put_pick(0, 0).start()

    @pl.loop(0, quads)
    def _(quad):
        for slot in range(2):
            pair = 2 * quad + slot
            fetch(pair).wait()

            @pl.when(pair >= 1)
            def _():
                put_pick(pair - 1, 1 - slot).wait()

            ats = [slice(k * edges, (k + 1) * edges) for k in range(2)]
            qs = [qin[2 * pair + k] for k in range(2)]
            scores = [dot_tn(picks[slot, :, ats[k]], qs[k]) for k in range(2)]
            spread(jnp.maximum(pair - 1, 0), 1 - slot)
            ds = []
            for k in range(2):
                tile = 2 * pair + k
                top = jnp.max(scores[k], axis=0, keepdims=True)
                expo = jnp.exp(scores[k] - top)
                probs = expo * (1.0 / jnp.sum(expo, axis=0, keepdims=True))
                d = jnp.where(eye, probs - 1.0, probs)
                if slot + k:
                    d = jnp.where(tile < live, d, 0.0)
                ds.append(d.astype(BF))
                diffs[tile] = ds[k]
            pick_tails(jnp.minimum(pair + 1, pairs - 1), 1 - slot)
            for k in range(2):
                moves[slot, :, ats[k]] = dot_nt(qs[k], ds[k]).astype(BF)
            put_diff(pair).start()

            @pl.when(pair + 1 < pairs)
            def _():
                put_pick(pair + 1, 1 - slot).start()

    spread(pairs - 1, 1)
    for chunk, at, row, lane in places(dim, rows, hub.shape[1], grads.shape[0]):
        grads[chunk, at] = acc[row : row + 8, lane : lane + LANES].astype(BF)
    for at in range(at + 1, grads.shape[1]):
        grads[chunk, at] = jnp.zeros((8, LANES), BF)
    put_pick(pairs - 1, 1).wait()

    @pl.loop(0, pairs)
    def _(pair):
        put_diff(pair).wait()


def head_kernel(count, pick, diff, weights, heads, ent, base, pin, din, moves, acc, psem, dsem, sem):
    half = acc.shape[0] // 2
    edges = heads.shape[1]
    live = count[0, 0]
    quads = (live + 3) // 4
    pairs = 2 * quads

    def get_pick(pair):
        return pltpu.make_async_copy(pick.at[pair], pin.at[pair], psem.at[pair])

    def get_diff(pair):
        both = pl.ds(2 * pair, 2)
        return pltpu.make_async_copy(diff.at[both], din.at[both], dsem.at[pair])

    @pl.loop(0, pairs)
    def _(pair):
        get_pick(pair).start()
        get_diff(pair).start()

    acc[...] = jnp.zeros_like(acc)
    moves[...] = jnp.zeros_like(moves)

    def spread(pair, slot):
        acc[...] += dot_nt(moves[slot], hot(pair_ids(heads, pair), acc.shape[1]))

    @pl.loop(0, quads)
    def _(quad):
        for slot in range(2):
            pair = 2 * quad + slot
            get_pick(pair).wait()
            get_diff(pair).wait()
            ats = [slice(k * edges, (k + 1) * edges) for k in range(2)]
            d_query = [dot_nn(pin[pair, :, ats[k]], din[2 * pair + k]) for k in range(2)]
            spread(jnp.maximum(pair - 1, 0), 1 - slot)
            for k in range(2):
                w = pick_lane(weights[...], 2 * pair + k)
                dr, di = d_query[k][:half], d_query[k][half:]
                wr, wi = w[:half], w[half:]
                moves[slot, :, ats[k]] = jnp.concatenate(
                    [dr * wr + di * wi, di * wr - dr * wi], axis=0
                ).astype(BF)

    spread(pairs - 1, 1)
    acc[...] = ent[...].astype(F32) - learn_rate * acc[...]
    put = pltpu.make_async_copy(acc, base.at[0], sem)
    put.start()
    put.wait()


def reorder_kernel(matching, rows, out, sems):
    puts = [
        pltpu.make_async_copy(rows.at[matching[g]], out.at[g], sems.at[g]) for g in range(out.shape[0])
    ]
    for put in puts:
        put.start()
    for put in puts:
        put.wait()


def return_kernel(matching, back, hub, out):
    own = out.shape[1] - hub.shape[1]
    total = hub[0].astype(F32)
    for m in range(1, hub.shape[0]):
        total += hub[m].astype(F32)
    total = total.astype(BF)
    for g in range(out.shape[0]):
        out[matching[g], :own] = back[g, :own]
        out[g, own:] = total


def update_kernel(base, hub, last, new_ent, new_hub, held, sems):
    dim, rows = new_ent.shape
    step = 80
    loads = [
        pltpu.make_async_copy(base.at[0, pl.ds(at, step)], held.at[pl.ds(at, step)], sems.at[i])
        for i, at in enumerate(range(0, dim, step))
    ]
    for load in loads:
        load.start()
    where = {(row, lane): (chunk, at) for chunk, at, row, lane in places(dim, rows, hub.shape[1], last.shape[0])}

    def got(row, lane):
        return jnp.concatenate([last[where[row, lane]], last[where[row + 8, lane]]], axis=0).astype(F32)

    for row in range(0, dim, 16):
        at = slice(row, row + 16)
        for lane in range(0, hub.shape[1], LANES):
            to = slice(lane, lane + LANES)
            new_hub[at, to] = (hub[at, to].astype(F32) - learn_rate * got(row, rows + lane)).astype(BF)
    for row in range(0, dim, 16):
        if row % step == 0:
            loads[row // step].wait()
        at = slice(row, row + 16)
        for lane in range(0, rows, LANES):
            to = slice(lane, lane + LANES)
            new_ent[at, to] = (held[at, to] - learn_rate * got(row, lane)).astype(BF)


def call(kernel, out_shape, in_specs, out_specs, flops, moved, scratch=(), exps=0, vmem=32, aliases={}):
    return pl.pallas_call(
        kernel,
        out_shape=out_shape,
        in_specs=in_specs,
        out_specs=out_specs,
        scratch_shapes=scratch,
        input_output_aliases=aliases,
        compiler_params=pltpu.CompilerParams(vmem_limit_bytes=vmem * 1024 * 1024),
        cost_estimate=pl.CostEstimate(flops=flops, bytes_accessed=moved, transcendentals=exps),
    )


shape = jax.ShapeDtypeStruct


def run_weights(tile_count, tile_rel, rel):
    dim, rels = rel.shape
    rest = rels % LANES or LANES
    return call(
        weight_kernel,
        shape((dim, LANES), F32),
        [SMEM, SMEM, HBM],
        VMEM,
        40 * dim * dim * dim,
        4 * rel.size,
        [pltpu.VMEM((dim, -(-rels // LANES) * LANES), F32), pltpu.VMEM((dim, rest), F32), DMA((2,))],
        vmem=60,
    )(tile_count, tile_rel, rel)


def run_query(tile_count, ent, head_index, weights):
    dim, rows = ent.shape
    tiles, edges = head_index.shape
    return call(
        query_kernel,
        shape((2 * tiles, dim, edges), BF),
        [SMEM, VMEM, VMEM, VMEM],
        HBM,
        2 * tiles * edges * dim * rows,
        2 * tiles * dim * edges,
        [pltpu.VMEM((tiles // 2, 2, dim, edges), BF), DMA((tiles // 2,))],
        vmem=60,
    )(tile_count, ent, head_index, weights)


def run_tail(tile_count, query, partner, hub, tail_index, groups):
    tiles, edges = tail_index.shape
    dim = query.shape[1]
    rows, hubs = partner.shape[1], hub.shape[1]
    return call(
        tail_kernel,
        [
            shape((tiles, dim, 2 * edges), BF),
            shape((3 * tiles, edges, edges), BF),
            shape((groups, sum(sizes(dim, rows, hubs, groups)), 8, LANES), BF),
        ],
        [SMEM, HBM, VMEM, VMEM, VMEM],
        [HBM, HBM, VMEM],
        4 * tiles * edges * dim * (rows + hubs + edges),
        8 * tiles * dim * edges,
        [
            pltpu.VMEM((dim, rows + hubs), BF),
            pltpu.VMEM((dim, rows + hubs), F32),
            pltpu.VMEM((tiles, dim, edges), BF),
            pltpu.VMEM((2, dim, 2 * edges), BF),
            pltpu.VMEM((tiles, edges, edges), BF),
            pltpu.VMEM((2, dim, 2 * edges), BF),
            DMA((tiles // 2,)),
            DMA((2,)),
            DMA((tiles // 2,)),
        ],
        tiles * edges * edges,
        vmem=50,
    )(tile_count, query, partner, hub, tail_index)


def run_head(tile_count, pick, diff, weights, head_index, ent):
    tiles, edges = head_index.shape
    dim, rows = ent.shape
    return call(
        head_kernel,
        shape((8, dim, rows), F32),
        [SMEM, HBM, HBM, VMEM, VMEM, VMEM],
        HBM,
        2 * tiles * edges * dim * (rows + edges),
        6 * tiles * dim * edges,
        [
            pltpu.VMEM((tiles // 2, dim, 2 * edges), BF),
            pltpu.VMEM((tiles, edges, edges), BF),
            pltpu.VMEM((2, dim, 2 * edges), BF),
            pltpu.VMEM((dim, rows), F32),
            DMA((tiles // 2,)),
            DMA((tiles // 2,)),
            DMA(()),
        ],
        vmem=60,
    )(tile_count, pick, diff, weights, head_index, ent)


def make(groups, members):
    def shards(entities, hub_rows, relations, matching, head_index, tail_index, tile_rel, tile_count):
        ent, hub, rel = entities.T, hub_rows.T, relations.T
        dim, rows = ent.shape
        hubs = hub.shape[1]
        own = sizes(dim, rows, hubs, groups)[0]

        high, wide = dim // 8, rows // LANES
        cut = ent.reshape(high, 8, wide, LANES).transpose(0, 2, 1, 3)
        cut = lax.all_to_all(cut.reshape(groups, -1, 8, LANES), "group", 0, 0)
        weights = run_weights(tile_count, tile_rel, rel)
        cut, weights = lax.optimization_barrier((cut, weights))
        cut = call(
            reorder_kernel, shape(cut.shape, BF), [SMEM, VMEM], HBM, 0, 4 * cut.size, [DMA((groups,))]
        )(matching, cut)
        partner = lax.all_to_all(cut, "group", 0, 0).reshape(high, wide, 8, LANES)
        partner = partner.transpose(0, 2, 1, 3).reshape(dim, rows)
        query = run_query(tile_count, ent, head_index, weights)
        pick, diff, grads = run_tail(tile_count, query, partner, hub, tail_index, groups)

        got = lax.all_to_all(grads, "group", 0, 0)
        got, pick, diff = lax.optimization_barrier((got, pick, diff))
        part = jnp.sum(got[:, own:].astype(F32), axis=0).astype(BF)
        other = lax.ppermute(part, "member", [(m, m ^ 1) for m in range(members)])
        part = (part.astype(F32) + other.astype(F32)).astype(BF)
        cores = [list(range(core, members, 2)) for core in range(2)]
        parts = jnp.broadcast_to(part[None], (members // 2,) + part.shape)
        parts = lax.all_to_all(parts, "member", 0, 0, axis_index_groups=cores)
        base = run_head(tile_count, pick, diff, weights, head_index, ent)
        parts, base = lax.optimization_barrier((parts, base))
        sent = call(
            return_kernel, shape(got.shape, BF), [SMEM, VMEM, VMEM], VMEM, 0, 4 * got.size
        )(matching, got, parts)
        last = lax.all_to_all(sent, "group", 0, 0)
        new_ent, new_hub = call(
            update_kernel,
            [shape((dim, rows), BF), shape((dim, hubs), BF)],
            [HBM, VMEM, VMEM],
            [VMEM, VMEM],
            0,
            8 * dim * rows,
            [pltpu.VMEM((dim, rows), F32), DMA((5,))],
            vmem=50,
        )(base, hub, last)
        return (new_ent.T, new_hub.T)

    return shards


def solution(mesh):
    placed = (
        P(("group", "member"), None),
        P(),
        P(),
        P(),
        P(("group", "member"), None),
        P(("group", "member"), None),
        P(("group", "member")),
        P("group", "member"),
    )
    return jax.shard_map(
        make(mesh.shape["group"], mesh.shape["member"]),
        mesh=mesh,
        in_specs=placed,
        out_specs=(P(("group", "member"), None), P()),
        check_vma=False,
    )
```

```python
import jax
import jax.numpy as jnp
from jax import lax
from jax.experimental import pallas as pl
from jax.experimental.pallas import tpu as pltpu
from jax.sharding import PartitionSpec as P

learn_rate = 0.1
BF = jnp.bfloat16
F32 = jnp.float32
LANES = 128
STEP = 80
HELD = 160
VMEM = pl.BlockSpec(memory_space=pltpu.VMEM)
SMEM = pl.BlockSpec(memory_space=pltpu.SMEM)
HBM = pl.BlockSpec(memory_space=pltpu.HBM)
DMA = pltpu.SemaphoreType.DMA


def hot(ids, rows):
    row = lax.broadcasted_iota(jnp.int32, (rows, ids.shape[1]), 0).astype(jnp.int16)
    return jnp.where(row == ids.astype(jnp.int16), jnp.ones((), BF), jnp.zeros((), BF))


def pair_ids(ids_ref, pair):
    return jnp.concatenate([ids_ref[pl.ds(2 * pair, 1), :], ids_ref[pl.ds(2 * pair + 1, 1), :]], axis=1)


def pick_lane(block, lane):
    lanes = lax.broadcasted_iota(jnp.int32, block.shape, 1)
    return jnp.sum(jnp.where(lanes == lane, block, 0.0), axis=1, keepdims=True)


def dot_nn(a, b):
    return lax.dot_general(a, b, (((1,), (0,)), ((), ())), preferred_element_type=F32)


def dot_nt(a, b):
    return lax.dot_general(a, b, (((1,), (1,)), ((), ())), preferred_element_type=F32)


def dot_tn(a, b):
    return lax.dot_general(a, b, (((0,), (0,)), ((), ())), preferred_element_type=F32)


def weight_kernel(count, rel_ids, rel, weights, table, last, sems):
    live = count[0, 0]
    whole = rel.shape[1] // LANES * LANES
    loads = [pltpu.make_async_copy(rel.at[:, pl.ds(0, whole)], table.at[:, pl.ds(0, whole)], sems.at[0])]
    if whole < rel.shape[1]:
        loads.append(pltpu.make_async_copy(rel.at[:, pl.ds(whole, rel.shape[1] - whole)], last, sems.at[1]))
    for load in loads:
        load.start()
    weights[...] = jnp.zeros_like(weights)
    for load in loads:
        load.wait()
    if whole < rel.shape[1]:
        table[:, whole : rel.shape[1]] = last[...]

    @pl.loop(0, (live + 1) // 2)
    def _(pair):
        total = weights[...]
        lanes = lax.broadcasted_iota(jnp.int32, weights.shape, 1)
        for k in range(2):
            tile = 2 * pair + k
            rid = rel_ids[tile]
            at = rid // LANES * LANES
            w = pick_lane(table[:, pl.ds(pl.multiple_of(at, LANES), LANES)], rid - at)
            total = jnp.where(lanes == tile, jnp.where(tile < live, w, 0.0), total)
        weights[...] = total


def query_kernel(count, ent, heads, weights, query, out, sems):
    live = count[0, 0]
    pairs = 2 * ((live + 3) // 4)
    half, edges = ent.shape[0] // 2, heads.shape[1]

    def put(pair):
        return pltpu.make_async_copy(out.at[pair], query.at[pl.ds(2 * pair, 2)], sems.at[pair])

    @pl.loop(0, pairs)
    def _(pair):
        head = dot_nn(ent[...], hot(pair_ids(heads, pair), ent.shape[1]))
        for k in range(2):
            w = pick_lane(weights[...], 2 * pair + k)
            hr = head[:half, k * edges : (k + 1) * edges]
            hi = head[half:, k * edges : (k + 1) * edges]
            wr, wi = w[:half], w[half:]
            out[pair, k] = jnp.concatenate([hr * wr - hi * wi, hr * wi + hi * wr], axis=0).astype(BF)
        put(pair).start()

    @pl.loop(0, pairs)
    def _(pair):
        put(pair).wait()


def sizes(dim, rows, hubs, chunks):
    return dim // 8 * (rows // LANES) // chunks, -(-(dim // 8 * (hubs // LANES)) // chunks)


def places(dim, rows, hubs, chunks):
    own, more = sizes(dim, rows, hubs, chunks)
    found = []
    for first, base, width, each in ((0, 0, rows, own), (own, rows, hubs, more)):
        wide = width // LANES
        for t in range(dim // 8 * wide):
            found.append((t // each, first + t % each, t // wide * 8, base + t % wide * LANES))
    return found


def tail_kernel(count, query, partner, hub, tails, pick, diff, grads, table, acc, qin, picks, diffs, moves, qsem, psem, dsem):
    dim, rows = hub.shape[0], partner.shape[1]
    edges = tails.shape[1]
    live = count[0, 0]
    quads = (live + 3) // 4
    pairs = 2 * quads

    def fetch(pair):
        both = pl.ds(2 * pair, 2)
        return pltpu.make_async_copy(query.at[both], qin.at[both], qsem.at[pair])

    def put_pick(pair, slot):
        return pltpu.make_async_copy(picks.at[slot], pick.at[pair], psem.at[slot])

    def put_diff(pair):
        both = pl.ds(2 * pair, 2)
        return pltpu.make_async_copy(diffs.at[both], diff.at[both], dsem.at[pair])

    @pl.loop(0, pairs)
    def _(pair):
        fetch(pair).start()

    table[:, :rows] = partner[:dim]
    table[:, rows:] = hub[...]
    acc[...] = jnp.zeros_like(acc)
    moves[...] = jnp.zeros_like(moves)
    eye = lax.broadcasted_iota(jnp.int32, (edges, edges), 0) == lax.broadcasted_iota(
        jnp.int32, (edges, edges), 1
    )

    def pick_tails(pair, slot):
        picks[slot] = dot_nn(table[...], hot(pair_ids(tails, pair), table.shape[1])).astype(BF)

    def spread(pair, slot):
        acc[...] += dot_nt(moves[slot], hot(pair_ids(tails, pair), table.shape[1]))

    pick_tails(0, 0)
    put_pick(0, 0).start()

    @pl.loop(0, quads)
    def _(quad):
        for slot in range(2):
            pair = 2 * quad + slot
            fetch(pair).wait()

            @pl.when(pair >= 1)
            def _():
                put_pick(pair - 1, 1 - slot).wait()

            ats = [slice(k * edges, (k + 1) * edges) for k in range(2)]
            qs = [qin[2 * pair + k] for k in range(2)]
            scores = [dot_tn(picks[slot, :, ats[k]], qs[k]) for k in range(2)]
            spread(jnp.maximum(pair - 1, 0), 1 - slot)
            ds = []
            for k in range(2):
                tile = 2 * pair + k
                top = jnp.max(scores[k], axis=0, keepdims=True)
                expo = jnp.exp(scores[k] - top)
                probs = expo * (1.0 / jnp.sum(expo, axis=0, keepdims=True))
                d = jnp.where(eye, probs - 1.0, probs)
                if slot + k:
                    d = jnp.where(tile < live, d, 0.0)
                ds.append(d.astype(BF))
                diffs[tile] = ds[k]
            pick_tails(jnp.minimum(pair + 1, pairs - 1), 1 - slot)
            for k in range(2):
                moves[slot, :, ats[k]] = dot_nt(qs[k], ds[k]).astype(BF)
            put_diff(pair).start()

            @pl.when(pair + 1 < pairs)
            def _():
                put_pick(pair + 1, 1 - slot).start()

    spread(pairs - 1, 1)
    for chunk, at, row, lane in places(dim, rows, hub.shape[1], grads.shape[0]):
        grads[chunk, at] = acc[row : row + 8, lane : lane + LANES].astype(BF)
    for at in range(at + 1, grads.shape[1]):
        grads[chunk, at] = jnp.zeros((8, LANES), BF)
    put_pick(pairs - 1, 1).wait()

    @pl.loop(0, pairs)
    def _(pair):
        put_diff(pair).wait()


def head_kernel(count, pick, diff, weights, heads, ent, base, pin, din, moves, acc, own, psem, dsem, own_sem, sems):
    half = acc.shape[0] // 2
    edges = heads.shape[1]
    live = count[0, 0]
    quads = (live + 3) // 4
    pairs = 2 * quads

    def get_pick(pair):
        return pltpu.make_async_copy(pick.at[pair], pin.at[pair], psem.at[pair])

    def get_diff(pair):
        both = pl.ds(2 * pair, 2)
        return pltpu.make_async_copy(diff.at[both], din.at[both], dsem.at[pair])

    @pl.loop(0, pairs)
    def _(pair):
        get_pick(pair).start()
        get_diff(pair).start()

    get_own = pltpu.make_async_copy(ent, own, own_sem)
    get_own.start()
    acc[...] = jnp.zeros_like(acc)
    moves[...] = jnp.zeros_like(moves)

    def spread(pair, slot):
        acc[...] += dot_nt(moves[slot], hot(pair_ids(heads, pair), acc.shape[1]))

    @pl.loop(0, quads)
    def _(quad):
        for slot in range(2):
            pair = 2 * quad + slot
            get_pick(pair).wait()
            get_diff(pair).wait()
            ats = [slice(k * edges, (k + 1) * edges) for k in range(2)]
            d_query = [dot_nn(pin[pair, :, ats[k]], din[2 * pair + k]) for k in range(2)]
            spread(jnp.maximum(pair - 1, 0), 1 - slot)
            for k in range(2):
                w = pick_lane(weights[...], 2 * pair + k)
                dr, di = d_query[k][:half], d_query[k][half:]
                wr, wi = w[:half], w[half:]
                moves[slot, :, ats[k]] = jnp.concatenate(
                    [dr * wr + di * wi, di * wr - dr * wi], axis=0
                ).astype(BF)

    spread(pairs - 1, 1)
    get_own.wait()
    puts = []
    for i, at in enumerate(range(0, acc.shape[0], STEP)):
        rng = slice(at, at + STEP)
        acc[rng] = own[rng].astype(F32) - learn_rate * acc[rng]
        puts.append(pltpu.make_async_copy(acc.at[pl.ds(at, STEP)], base.at[0, pl.ds(at, STEP)], sems.at[i]))
        puts[i].start()
    for put in puts:
        put.wait()


def reorder_kernel(matching, rows, out, sems):
    puts = [
        pltpu.make_async_copy(rows.at[matching[g]], out.at[g], sems.at[g]) for g in range(out.shape[0])
    ]
    for put in puts:
        put.start()
    for put in puts:
        put.wait()


def return_kernel(matching, back, hub, base, out, held, sem):
    load = pltpu.make_async_copy(base.at[0, pl.ds(0, HELD)], held, sem)
    load.start()
    own = out.shape[1] - hub.shape[1]
    total = hub[0].astype(F32)
    for m in range(1, hub.shape[0]):
        total += hub[m].astype(F32)
    total = total.astype(BF)
    for g in range(out.shape[0]):
        out[matching[g], :own] = back[g, :own]
        out[g, own:] = total
    load.wait()


def update_kernel(base, held, hub, last, new_ent, new_hub, more, ent_out, hub_out, get_sems, put_sems, hub_sem):
    dim, rows = ent_out.shape
    loads = {
        at: pltpu.make_async_copy(
            base.at[0, pl.ds(at, STEP)], more.at[pl.ds(at - HELD, STEP)], get_sems.at[i]
        )
        for i, at in enumerate(range(HELD, dim, STEP))
    }
    for load in loads.values():
        load.start()
    where = {(row, lane): (chunk, at) for chunk, at, row, lane in places(dim, rows, hub.shape[1], last.shape[0])}

    def got(row, lane):
        return jnp.concatenate([last[where[row, lane]], last[where[row + 8, lane]]], axis=0).astype(F32)

    for row in range(0, dim, 16):
        at = slice(row, row + 16)
        for lane in range(0, hub.shape[1], LANES):
            to = slice(lane, lane + LANES)
            hub_out[at, to] = (hub[at, to].astype(F32) - learn_rate * got(row, rows + lane)).astype(BF)
    put_hub = pltpu.make_async_copy(hub_out, new_hub, hub_sem)
    put_hub.start()
    puts = []
    for i, first in enumerate(range(0, dim, STEP)):
        if first in loads:
            loads[first].wait()
        for row in range(first, first + STEP, 16):
            for lane in range(0, rows, LANES):
                to = slice(lane, lane + LANES)
                old = held[row : row + 16, to] if row < HELD else more[row - HELD : row - HELD + 16, to]
                ent_out[row : row + 16, to] = (old - learn_rate * got(row, lane)).astype(BF)
        rng = pl.ds(first, STEP)
        puts.append(pltpu.make_async_copy(ent_out.at[rng], new_ent.at[rng], put_sems.at[i]))
        puts[i].start()
    for put in puts:
        put.wait()
    put_hub.wait()


def call(kernel, out_shape, in_specs, out_specs, flops, moved, scratch=(), exps=0, vmem=32, aliases={}):
    return pl.pallas_call(
        kernel,
        out_shape=out_shape,
        in_specs=in_specs,
        out_specs=out_specs,
        scratch_shapes=scratch,
        input_output_aliases=aliases,
        compiler_params=pltpu.CompilerParams(vmem_limit_bytes=vmem * 1024 * 1024),
        cost_estimate=pl.CostEstimate(flops=flops, bytes_accessed=moved, transcendentals=exps),
    )


shape = jax.ShapeDtypeStruct


def run_weights(tile_count, tile_rel, rel):
    dim, rels = rel.shape
    rest = rels % LANES or LANES
    return call(
        weight_kernel,
        shape((dim, LANES), F32),
        [SMEM, SMEM, HBM],
        VMEM,
        40 * dim * dim * dim,
        4 * rel.size,
        [pltpu.VMEM((dim, -(-rels // LANES) * LANES), F32), pltpu.VMEM((dim, rest), F32), DMA((2,))],
        vmem=60,
    )(tile_count, tile_rel, rel)


def run_query(tile_count, ent, head_index, weights):
    dim, rows = ent.shape
    tiles, edges = head_index.shape
    return call(
        query_kernel,
        shape((2 * tiles, dim, edges), BF),
        [SMEM, VMEM, VMEM, VMEM],
        HBM,
        2 * tiles * edges * dim * rows,
        2 * tiles * dim * edges,
        [pltpu.VMEM((tiles // 2, 2, dim, edges), BF), DMA((tiles // 2,))],
        vmem=60,
    )(tile_count, ent, head_index, weights)


def run_tail(tile_count, query, partner, hub, tail_index, groups):
    tiles, edges = tail_index.shape
    dim = query.shape[1]
    rows, hubs = partner.shape[1], hub.shape[1]
    return call(
        tail_kernel,
        [
            shape((tiles, dim, 2 * edges), BF),
            shape((3 * tiles, edges, edges), BF),
            shape((groups, sum(sizes(dim, rows, hubs, groups)), 8, LANES), BF),
        ],
        [SMEM, HBM, VMEM, VMEM, VMEM],
        [HBM, HBM, VMEM],
        4 * tiles * edges * dim * (rows + hubs + edges),
        8 * tiles * dim * edges,
        [
            pltpu.VMEM((dim, rows + hubs), BF),
            pltpu.VMEM((dim, rows + hubs), F32),
            pltpu.VMEM((tiles, dim, edges), BF),
            pltpu.VMEM((2, dim, 2 * edges), BF),
            pltpu.VMEM((tiles, edges, edges), BF),
            pltpu.VMEM((2, dim, 2 * edges), BF),
            DMA((tiles // 2,)),
            DMA((2,)),
            DMA((tiles // 2,)),
        ],
        tiles * edges * edges,
        vmem=50,
    )(tile_count, query, partner, hub, tail_index)


def run_head(tile_count, pick, diff, weights, head_index, ent):
    tiles, edges = head_index.shape
    dim, rows = ent.shape
    return call(
        head_kernel,
        shape((8, dim, rows), F32),
        [SMEM, HBM, HBM, VMEM, VMEM, HBM],
        HBM,
        2 * tiles * edges * dim * (rows + edges),
        6 * tiles * dim * edges,
        [
            pltpu.VMEM((tiles // 2, dim, 2 * edges), BF),
            pltpu.VMEM((tiles, edges, edges), BF),
            pltpu.VMEM((2, dim, 2 * edges), BF),
            pltpu.VMEM((dim, rows), F32),
            pltpu.VMEM((dim, rows), BF),
            DMA((tiles // 2,)),
            DMA((tiles // 2,)),
            DMA(()),
            DMA((dim // STEP,)),
        ],
        vmem=60,
    )(tile_count, pick, diff, weights, head_index, ent)


def make(groups, members):
    def shards(entities, hub_rows, relations, matching, head_index, tail_index, tile_rel, tile_count):
        ent, hub, rel = entities.T, hub_rows.T, relations.T
        dim, rows = ent.shape
        hubs = hub.shape[1]
        own = sizes(dim, rows, hubs, groups)[0]

        high, wide = dim // 8, rows // LANES
        cut = ent.reshape(high, 8, wide, LANES).transpose(0, 2, 1, 3)
        cut = lax.all_to_all(cut.reshape(groups, -1, 8, LANES), "group", 0, 0)
        weights = run_weights(tile_count, tile_rel, rel)
        cut, weights = lax.optimization_barrier((cut, weights))
        cut = call(
            reorder_kernel, shape(cut.shape, BF), [SMEM, VMEM], HBM, 0, 4 * cut.size, [DMA((groups,))]
        )(matching, cut)
        partner = lax.all_to_all(cut, "group", 0, 0).reshape(high, wide, 8, LANES)
        partner = partner.transpose(0, 2, 1, 3).reshape(dim, rows)
        query = run_query(tile_count, ent, head_index, weights)
        pick, diff, grads = run_tail(tile_count, query, partner, hub, tail_index, groups)

        got = lax.all_to_all(grads, "group", 0, 0)
        got, pick, diff = lax.optimization_barrier((got, pick, diff))
        part = jnp.sum(got[:, own:].astype(F32), axis=0).astype(BF)
        other = lax.ppermute(part, "member", [(m, m ^ 1) for m in range(members)])
        part = (part.astype(F32) + other.astype(F32)).astype(BF)
        cores = [list(range(core, members, 2)) for core in range(2)]
        parts = jnp.broadcast_to(part[None], (members // 2,) + part.shape)
        parts = lax.all_to_all(parts, "member", 0, 0, axis_index_groups=cores)
        base = run_head(tile_count, pick, diff, weights, head_index, ent)
        parts, base = lax.optimization_barrier((parts, base))
        sent, held = call(
            return_kernel,
            [shape(got.shape, BF), shape((HELD, rows), F32)],
            [SMEM, VMEM, VMEM, HBM],
            [VMEM, VMEM],
            0,
            4 * got.size,
            [DMA(())],
            vmem=50,
        )(matching, got, parts, base)
        last = lax.all_to_all(sent, "group", 0, 0)
        new_ent, new_hub = call(
            update_kernel,
            [shape((dim, rows), BF), shape((dim, hubs), BF)],
            [HBM, VMEM, VMEM, VMEM],
            [HBM, HBM],
            0,
            8 * dim * rows,
            [
                pltpu.VMEM((dim - HELD, rows), F32),
                pltpu.VMEM((dim, rows), BF),
                pltpu.VMEM((dim, hubs), BF),
                DMA(((dim - HELD) // STEP,)),
                DMA((dim // STEP,)),
                DMA(()),
            ],
            vmem=50,
        )(base, held, hub, last)
        return (new_ent.T, new_hub.T)

    return shards


def solution(mesh):
    placed = (
        P(("group", "member"), None),
        P(),
        P(),
        P(),
        P(("group", "member"), None),
        P(("group", "member"), None),
        P(("group", "member")),
        P("group", "member"),
    )
    return jax.shard_map(
        make(mesh.shape["group"], mesh.shape["member"]),
        mesh=mesh,
        in_specs=placed,
        out_specs=(P(("group", "member"), None), P()),
        check_vma=False,
    )
```

```python
import jax
import jax.numpy as jnp
from jax import lax
from jax.experimental import pallas as pl
from jax.experimental.pallas import tpu as pltpu
from jax.sharding import PartitionSpec as P

learn_rate = 0.1
BF = jnp.bfloat16
F32 = jnp.float32
LANES = 128
VMEM = pl.BlockSpec(memory_space=pltpu.VMEM)
SMEM = pl.BlockSpec(memory_space=pltpu.SMEM)
HBM = pl.BlockSpec(memory_space=pltpu.HBM)
DMA = pltpu.SemaphoreType.DMA


def hot(ids, rows):
    row = lax.broadcasted_iota(jnp.int32, (rows, ids.shape[1]), 0).astype(jnp.int16)
    return jnp.where(row == ids.astype(jnp.int16), jnp.ones((), BF), jnp.zeros((), BF))


def pair_ids(ids_ref, pair):
    return jnp.concatenate([ids_ref[pl.ds(2 * pair, 1), :], ids_ref[pl.ds(2 * pair + 1, 1), :]], axis=1)


def pick_lane(block, lane):
    lanes = lax.broadcasted_iota(jnp.int32, block.shape, 1)
    return jnp.sum(jnp.where(lanes == lane, block, 0.0), axis=1, keepdims=True)


def dot_nn(a, b):
    return lax.dot_general(a, b, (((1,), (0,)), ((), ())), preferred_element_type=F32)


def dot_nt(a, b):
    return lax.dot_general(a, b, (((1,), (1,)), ((), ())), preferred_element_type=F32)


def dot_tn(a, b):
    return lax.dot_general(a, b, (((0,), (0,)), ((), ())), preferred_element_type=F32)


def weight_kernel(count, rel_ids, rel, weights, table, last, sems):
    live = count[0, 0]
    whole = rel.shape[1] // LANES * LANES
    loads = [pltpu.make_async_copy(rel.at[:, pl.ds(0, whole)], table.at[:, pl.ds(0, whole)], sems.at[0])]
    if whole < rel.shape[1]:
        loads.append(pltpu.make_async_copy(rel.at[:, pl.ds(whole, rel.shape[1] - whole)], last, sems.at[1]))
    for load in loads:
        load.start()
    weights[...] = jnp.zeros_like(weights)
    for load in loads:
        load.wait()
    if whole < rel.shape[1]:
        table[:, whole : rel.shape[1]] = last[...]

    @pl.loop(0, (live + 1) // 2)
    def _(pair):
        total = weights[...]
        lanes = lax.broadcasted_iota(jnp.int32, weights.shape, 1)
        for k in range(2):
            tile = 2 * pair + k
            rid = rel_ids[tile]
            at = rid // LANES * LANES
            w = pick_lane(table[:, pl.ds(pl.multiple_of(at, LANES), LANES)], rid - at)
            total = jnp.where(lanes == tile, jnp.where(tile < live, w, 0.0), total)
        weights[...] = total


def query_kernel(count, ent, heads, weights, query, out, sems):
    live = count[0, 0]
    pairs = 2 * ((live + 3) // 4)
    half, edges = ent.shape[0] // 2, heads.shape[1]

    def put(pair):
        return pltpu.make_async_copy(out.at[pair], query.at[pl.ds(2 * pair, 2)], sems.at[pair])

    @pl.loop(0, pairs)
    def _(pair):
        head = dot_nn(ent[...], hot(pair_ids(heads, pair), ent.shape[1]))
        for k in range(2):
            w = pick_lane(weights[...], 2 * pair + k)
            hr = head[:half, k * edges : (k + 1) * edges]
            hi = head[half:, k * edges : (k + 1) * edges]
            wr, wi = w[:half], w[half:]
            out[pair, k] = jnp.concatenate([hr * wr - hi * wi, hr * wi + hi * wr], axis=0).astype(BF)
        put(pair).start()

    @pl.loop(0, pairs)
    def _(pair):
        put(pair).wait()


def sizes(dim, rows, hubs, chunks):
    return dim // 8 * (rows // LANES) // chunks, -(-(dim // 8 * (hubs // LANES)) // chunks)


def places(dim, rows, hubs, chunks):
    own, more = sizes(dim, rows, hubs, chunks)
    found = []
    for first, base, width, each in ((0, 0, rows, own), (own, rows, hubs, more)):
        wide = width // LANES
        for t in range(dim // 8 * wide):
            found.append((t // each, first + t % each, t // wide * 8, base + t % wide * LANES))
    return found


def tail_kernel(count, query, partner, hub, tails, pick, diff, grads, table, acc, qin, picks, diffs, moves, qsem, psem, dsem):
    dim, rows = hub.shape[0], partner.shape[1]
    edges = tails.shape[1]
    live = count[0, 0]
    quads = (live + 3) // 4
    pairs = 2 * quads

    def fetch(pair):
        both = pl.ds(2 * pair, 2)
        return pltpu.make_async_copy(query.at[both], qin.at[both], qsem.at[pair])

    def put_pick(pair, slot):
        return pltpu.make_async_copy(picks.at[slot], pick.at[pair], psem.at[slot])

    def put_diff(pair):
        both = pl.ds(2 * pair, 2)
        return pltpu.make_async_copy(diffs.at[both], diff.at[both], dsem.at[pair])

    @pl.loop(0, pairs)
    def _(pair):
        fetch(pair).start()

    table[:, :rows] = partner[:dim]
    table[:, rows:] = hub[...]
    acc[...] = jnp.zeros_like(acc)
    moves[...] = jnp.zeros_like(moves)
    eye = lax.broadcasted_iota(jnp.int32, (edges, edges), 0) == lax.broadcasted_iota(
        jnp.int32, (edges, edges), 1
    )

    def pick_tails(pair, slot):
        picks[slot] = dot_nn(table[...], hot(pair_ids(tails, pair), table.shape[1])).astype(BF)

    def spread(pair, slot):
        acc[...] += dot_nt(moves[slot], hot(pair_ids(tails, pair), table.shape[1]))

    pick_tails(0, 0)
    put_pick(0, 0).start()

    @pl.loop(0, quads)
    def _(quad):
        for slot in range(2):
            pair = 2 * quad + slot
            fetch(pair).wait()

            @pl.when(pair >= 1)
            def _():
                put_pick(pair - 1, 1 - slot).wait()

            ats = [slice(k * edges, (k + 1) * edges) for k in range(2)]
            qs = [qin[2 * pair + k] for k in range(2)]
            scores = [dot_tn(picks[slot, :, ats[k]], qs[k]) for k in range(2)]
            spread(jnp.maximum(pair - 1, 0), 1 - slot)
            ds = []
            for k in range(2):
                tile = 2 * pair + k
                top = jnp.max(scores[k], axis=0, keepdims=True)
                expo = jnp.exp(scores[k] - top)
                probs = expo * (1.0 / jnp.sum(expo, axis=0, keepdims=True))
                d = jnp.where(eye, probs - 1.0, probs)
                if slot + k:
                    d = jnp.where(tile < live, d, 0.0)
                ds.append(d.astype(BF))
                diffs[tile] = ds[k]
            pick_tails(jnp.minimum(pair + 1, pairs - 1), 1 - slot)
            for k in range(2):
                moves[slot, :, ats[k]] = dot_nt(qs[k], ds[k]).astype(BF)
            put_diff(pair).start()

            @pl.when(pair + 1 < pairs)
            def _():
                put_pick(pair + 1, 1 - slot).start()

    spread(pairs - 1, 1)
    for chunk, at, row, lane in places(dim, rows, hub.shape[1], grads.shape[0]):
        grads[chunk, at] = acc[row : row + 8, lane : lane + LANES].astype(BF)
    for at in range(at + 1, grads.shape[1]):
        grads[chunk, at] = jnp.zeros((8, LANES), BF)
    put_pick(pairs - 1, 1).wait()

    @pl.loop(0, pairs)
    def _(pair):
        put_diff(pair).wait()


def head_kernel(count, pick, diff, weights, heads, ent, acc, pin, din, moves, own, psem, dsem, sem):
    half = acc.shape[0] // 2
    edges = heads.shape[1]
    live = count[0, 0]
    quads = (live + 3) // 4
    pairs = 2 * quads

    def get_pick(pair):
        return pltpu.make_async_copy(pick.at[pair], pin.at[pair], psem.at[pair])

    def get_diff(pair):
        both = pl.ds(2 * pair, 2)
        return pltpu.make_async_copy(diff.at[both], din.at[both], dsem.at[pair])

    @pl.loop(0, pairs)
    def _(pair):
        get_pick(pair).start()
        get_diff(pair).start()

    get_own = pltpu.make_async_copy(ent, own, sem)
    get_own.start()
    acc[...] = jnp.zeros_like(acc)
    moves[...] = jnp.zeros_like(moves)

    def spread(pair, slot):
        acc[...] += dot_nt(moves[slot], hot(pair_ids(heads, pair), acc.shape[1]))

    @pl.loop(0, quads)
    def _(quad):
        for slot in range(2):
            pair = 2 * quad + slot
            get_pick(pair).wait()
            get_diff(pair).wait()
            ats = [slice(k * edges, (k + 1) * edges) for k in range(2)]
            d_query = [dot_nn(pin[pair, :, ats[k]], din[2 * pair + k]) for k in range(2)]
            spread(jnp.maximum(pair - 1, 0), 1 - slot)
            for k in range(2):
                w = pick_lane(weights[...], 2 * pair + k)
                dr, di = d_query[k][:half], d_query[k][half:]
                wr, wi = w[:half], w[half:]
                moves[slot, :, ats[k]] = jnp.concatenate(
                    [dr * wr + di * wi, di * wr - dr * wi], axis=0
                ).astype(BF)

    spread(pairs - 1, 1)
    get_own.wait()
    acc[...] = own[...].astype(F32) - learn_rate * acc[...]


def reorder_kernel(matching, rows, out, sems):
    puts = [
        pltpu.make_async_copy(rows.at[matching[g]], out.at[g], sems.at[g]) for g in range(out.shape[0])
    ]
    for put in puts:
        put.start()
    for put in puts:
        put.wait()


def return_kernel(matching, back, hub, out):
    own = out.shape[1] - hub.shape[1]
    total = hub[0].astype(F32)
    for m in range(1, hub.shape[0]):
        total += hub[m].astype(F32)
    total = total.astype(BF)
    for g in range(out.shape[0]):
        out[matching[g], :own] = back[g, :own]
        out[g, own:] = total


def update_kernel(base, hub, last, new_ent, new_hub):
    dim, rows = base.shape
    where = {(row, lane): (chunk, at) for chunk, at, row, lane in places(dim, rows, hub.shape[1], last.shape[0])}

    def got(row, lane):
        return jnp.concatenate([last[where[row, lane]], last[where[row + 8, lane]]], axis=0).astype(F32)

    for row in range(0, dim, 16):
        at = slice(row, row + 16)
        for lane in range(0, rows, LANES):
            to = slice(lane, lane + LANES)
            new_ent[at, to] = (base[at, to] - learn_rate * got(row, lane)).astype(BF)
        for lane in range(0, hub.shape[1], LANES):
            to = slice(lane, lane + LANES)
            new_hub[at, to] = (hub[at, to].astype(F32) - learn_rate * got(row, rows + lane)).astype(BF)


def call(kernel, out_shape, in_specs, out_specs, flops, moved, scratch=(), exps=0, vmem=32, aliases={}):
    return pl.pallas_call(
        kernel,
        out_shape=out_shape,
        in_specs=in_specs,
        out_specs=out_specs,
        scratch_shapes=scratch,
        input_output_aliases=aliases,
        compiler_params=pltpu.CompilerParams(vmem_limit_bytes=vmem * 1024 * 1024),
        cost_estimate=pl.CostEstimate(flops=flops, bytes_accessed=moved, transcendentals=exps),
    )


shape = jax.ShapeDtypeStruct


def run_weights(tile_count, tile_rel, rel):
    dim, rels = rel.shape
    rest = rels % LANES or LANES
    return call(
        weight_kernel,
        shape((dim, LANES), F32),
        [SMEM, SMEM, HBM],
        VMEM,
        40 * dim * dim * dim,
        4 * rel.size,
        [pltpu.VMEM((dim, -(-rels // LANES) * LANES), F32), pltpu.VMEM((dim, rest), F32), DMA((2,))],
        vmem=60,
    )(tile_count, tile_rel, rel)


def run_query(tile_count, ent, head_index, weights):
    dim, rows = ent.shape
    tiles, edges = head_index.shape
    return call(
        query_kernel,
        shape((2 * tiles, dim, edges), BF),
        [SMEM, VMEM, VMEM, VMEM],
        HBM,
        2 * tiles * edges * dim * rows,
        2 * tiles * dim * edges,
        [pltpu.VMEM((tiles // 2, 2, dim, edges), BF), DMA((tiles // 2,))],
        vmem=60,
    )(tile_count, ent, head_index, weights)


def run_tail(tile_count, query, partner, hub, tail_index, groups):
    tiles, edges = tail_index.shape
    dim = query.shape[1]
    rows, hubs = partner.shape[1], hub.shape[1]
    return call(
        tail_kernel,
        [
            shape((tiles, dim, 2 * edges), BF),
            shape((3 * tiles, edges, edges), BF),
            shape((groups, sum(sizes(dim, rows, hubs, groups)), 8, LANES), BF),
        ],
        [SMEM, HBM, VMEM, VMEM, VMEM],
        [HBM, HBM, VMEM],
        4 * tiles * edges * dim * (rows + hubs + edges),
        8 * tiles * dim * edges,
        [
            pltpu.VMEM((dim, rows + hubs), BF),
            pltpu.VMEM((dim, rows + hubs), F32),
            pltpu.VMEM((tiles, dim, edges), BF),
            pltpu.VMEM((2, dim, 2 * edges), BF),
            pltpu.VMEM((tiles, edges, edges), BF),
            pltpu.VMEM((2, dim, 2 * edges), BF),
            DMA((tiles // 2,)),
            DMA((2,)),
            DMA((tiles // 2,)),
        ],
        tiles * edges * edges,
        vmem=50,
    )(tile_count, query, partner, hub, tail_index)


def run_head(tile_count, pick, diff, weights, head_index, ent):
    tiles, edges = head_index.shape
    dim, rows = ent.shape
    return call(
        head_kernel,
        shape((dim, rows), F32),
        [SMEM, HBM, HBM, VMEM, VMEM, HBM],
        VMEM,
        2 * tiles * edges * dim * (rows + edges),
        6 * tiles * dim * edges,
        [
            pltpu.VMEM((tiles // 2, dim, 2 * edges), BF),
            pltpu.VMEM((tiles, edges, edges), BF),
            pltpu.VMEM((2, dim, 2 * edges), BF),
            pltpu.VMEM((dim, rows), BF),
            DMA((tiles // 2,)),
            DMA((tiles // 2,)),
            DMA(()),
        ],
        vmem=50,
    )(tile_count, pick, diff, weights, head_index, ent)


def make(groups, members):
    def shards(entities, hub_rows, relations, matching, head_index, tail_index, tile_rel, tile_count):
        ent, hub, rel = entities.T, hub_rows.T, relations.T
        dim, rows = ent.shape
        hubs = hub.shape[1]
        own = sizes(dim, rows, hubs, groups)[0]

        high, wide = dim // 8, rows // LANES
        cut = ent.reshape(high, 8, wide, LANES).transpose(0, 2, 1, 3)
        cut = lax.all_to_all(cut.reshape(groups, -1, 8, LANES), "group", 0, 0)
        weights = run_weights(tile_count, tile_rel, rel)
        cut, weights = lax.optimization_barrier((cut, weights))
        cut = call(
            reorder_kernel, shape(cut.shape, BF), [SMEM, VMEM], HBM, 0, 4 * cut.size, [DMA((groups,))]
        )(matching, cut)
        partner = lax.all_to_all(cut, "group", 0, 0).reshape(high, wide, 8, LANES)
        partner = partner.transpose(0, 2, 1, 3).reshape(dim, rows)
        query = run_query(tile_count, ent, head_index, weights)
        pick, diff, grads = run_tail(tile_count, query, partner, hub, tail_index, groups)

        got = lax.all_to_all(grads, "group", 0, 0)
        got, pick, diff = lax.optimization_barrier((got, pick, diff))
        part = jnp.sum(got[:, own:].astype(F32), axis=0).astype(BF)
        other = lax.ppermute(part, "member", [(m, m ^ 1) for m in range(members)])
        part = (part.astype(F32) + other.astype(F32)).astype(BF)
        cores = [list(range(core, members, 2)) for core in range(2)]
        parts = jnp.broadcast_to(part[None], (members // 2,) + part.shape)
        parts = lax.all_to_all(parts, "member", 0, 0, axis_index_groups=cores)
        base = run_head(tile_count, pick, diff, weights, head_index, ent)
        parts, base = lax.optimization_barrier((parts, base))
        sent = call(
            return_kernel, shape(got.shape, BF), [SMEM, VMEM, VMEM], VMEM, 0, 4 * got.size
        )(matching, got, parts)
        last = lax.all_to_all(sent, "group", 0, 0)
        new_ent, new_hub = call(
            update_kernel,
            [shape((dim, rows), BF), shape((dim, hubs), BF)],
            [VMEM, VMEM, VMEM],
            [VMEM, VMEM],
            0,
            8 * dim * rows,
        )(base, hub, last)
        return (new_ent.T, new_hub.T)

    return shards


def solution(mesh):
    placed = (
        P(("group", "member"), None),
        P(),
        P(),
        P(),
        P(("group", "member"), None),
        P(("group", "member"), None),
        P(("group", "member")),
        P("group", "member"),
    )
    return jax.shard_map(
        make(mesh.shape["group"], mesh.shape["member"]),
        mesh=mesh,
        in_specs=placed,
        out_specs=(P(("group", "member"), None), P()),
        check_vma=False,
    )
```

```python
import jax
import jax.numpy as jnp
from jax import lax
from jax.experimental import pallas as pl
from jax.experimental.pallas import tpu as pltpu
from jax.sharding import PartitionSpec as P

learn_rate = 0.1
BF = jnp.bfloat16
F32 = jnp.float32
LANES = 128
VMEM = pl.BlockSpec(memory_space=pltpu.VMEM)
SMEM = pl.BlockSpec(memory_space=pltpu.SMEM)
HBM = pl.BlockSpec(memory_space=pltpu.HBM)
DMA = pltpu.SemaphoreType.DMA


def hot(ids, rows):
    row = lax.broadcasted_iota(jnp.int32, (rows, ids.shape[1]), 0).astype(jnp.int16)
    return jnp.where(row == ids.astype(jnp.int16), jnp.ones((), BF), jnp.zeros((), BF))


def pair_ids(ids_ref, pair):
    return jnp.concatenate([ids_ref[pl.ds(2 * pair, 1), :], ids_ref[pl.ds(2 * pair + 1, 1), :]], axis=1)


def pick_lane(block, lane):
    lanes = lax.broadcasted_iota(jnp.int32, block.shape, 1)
    return jnp.sum(jnp.where(lanes == lane, block, 0.0), axis=1, keepdims=True)


def dot_nn(a, b):
    return lax.dot_general(a, b, (((1,), (0,)), ((), ())), preferred_element_type=F32)


def dot_nt(a, b):
    return lax.dot_general(a, b, (((1,), (1,)), ((), ())), preferred_element_type=F32)


def dot_tn(a, b):
    return lax.dot_general(a, b, (((0,), (0,)), ((), ())), preferred_element_type=F32)


def weight_kernel(count, rel_ids, rel, weights, table, last, sems):
    live = count[0, 0]
    whole = rel.shape[1] // LANES * LANES
    loads = [pltpu.make_async_copy(rel.at[:, pl.ds(0, whole)], table.at[:, pl.ds(0, whole)], sems.at[0])]
    if whole < rel.shape[1]:
        loads.append(pltpu.make_async_copy(rel.at[:, pl.ds(whole, rel.shape[1] - whole)], last, sems.at[1]))
    for load in loads:
        load.start()
    weights[...] = jnp.zeros_like(weights)
    for load in loads:
        load.wait()
    if whole < rel.shape[1]:
        table[:, whole : rel.shape[1]] = last[...]

    @pl.loop(0, (live + 1) // 2)
    def _(pair):
        total = weights[...]
        lanes = lax.broadcasted_iota(jnp.int32, weights.shape, 1)
        for k in range(2):
            tile = 2 * pair + k
            rid = rel_ids[tile]
            at = rid // LANES * LANES
            w = pick_lane(table[:, pl.ds(pl.multiple_of(at, LANES), LANES)], rid - at)
            total = jnp.where(lanes == tile, jnp.where(tile < live, w, 0.0), total)
        weights[...] = total


def query_kernel(count, ent, heads, weights, query, first, out, sems):
    live = count[0, 0]
    pairs = 2 * ((live + 3) // 4)
    half, edges = ent.shape[0] // 2, heads.shape[1]

    def put(pair):
        return pltpu.make_async_copy(out.at[pair], query.at[pl.ds(2 * pair, 2)], sems.at[pair])

    @pl.loop(0, pairs)
    def _(pair):
        head = dot_nn(ent[...], hot(pair_ids(heads, pair), ent.shape[1]))
        for k in range(2):
            w = pick_lane(weights[...], 2 * pair + k)
            hr = head[:half, k * edges : (k + 1) * edges]
            hi = head[half:, k * edges : (k + 1) * edges]
            wr, wi = w[:half], w[half:]
            out[pair, k] = jnp.concatenate([hr * wr - hi * wi, hr * wi + hi * wr], axis=0).astype(BF)
        put(pair).start()

    first[...] = out[0]

    @pl.loop(0, pairs)
    def _(pair):
        put(pair).wait()


def sizes(dim, rows, hubs, chunks):
    return dim // 8 * (rows // LANES) // chunks, -(-(dim // 8 * (hubs // LANES)) // chunks)


def places(dim, rows, hubs, chunks):
    own, more = sizes(dim, rows, hubs, chunks)
    found = []
    for first, base, width, each in ((0, 0, rows, own), (own, rows, hubs, more)):
        wide = width // LANES
        for t in range(dim // 8 * wide):
            found.append((t // each, first + t % each, t // wide * 8, base + t % wide * LANES))
    return found


def tail_kernel(count, query, first, partner, hub, tails, pick, diff, grads, table, acc, qin, picks, diffs, moves, qsem, psem, dsem):
    dim, rows = hub.shape[0], partner.shape[1]
    edges = tails.shape[1]
    live = count[0, 0]
    quads = (live + 3) // 4
    pairs = 2 * quads

    def fetch(pair):
        both = pl.ds(2 * pair, 2)
        return pltpu.make_async_copy(query.at[both], qin.at[both], qsem.at[pair])

    def put_pick(pair, slot):
        return pltpu.make_async_copy(picks.at[slot], pick.at[pair], psem.at[slot])

    def put_diff(pair):
        both = pl.ds(2 * pair, 2)
        return pltpu.make_async_copy(diffs.at[both], diff.at[both], dsem.at[pair])

    @pl.loop(1, pairs)
    def _(pair):
        fetch(pair).start()

    qin[:2] = first[...]
    table[:, :rows] = partner[:dim]
    table[:, rows:] = hub[...]
    acc[...] = jnp.zeros_like(acc)
    moves[...] = jnp.zeros_like(moves)
    eye = lax.broadcasted_iota(jnp.int32, (edges, edges), 0) == lax.broadcasted_iota(
        jnp.int32, (edges, edges), 1
    )

    def pick_tails(pair, slot):
        picks[slot] = dot_nn(table[...], hot(pair_ids(tails, pair), table.shape[1])).astype(BF)

    def spread(pair, slot):
        acc[...] += dot_nt(moves[slot], hot(pair_ids(tails, pair), table.shape[1]))

    pick_tails(0, 0)
    put_pick(0, 0).start()

    @pl.loop(0, quads)
    def _(quad):
        for slot in range(2):
            pair = 2 * quad + slot
            @pl.when(pair >= 1)
            def _():
                fetch(pair).wait()
                put_pick(pair - 1, 1 - slot).wait()

            ats = [slice(k * edges, (k + 1) * edges) for k in range(2)]
            qs = [qin[2 * pair + k] for k in range(2)]
            scores = [dot_tn(picks[slot, :, ats[k]], qs[k]) for k in range(2)]
            spread(jnp.maximum(pair - 1, 0), 1 - slot)
            ds = []
            for k in range(2):
                tile = 2 * pair + k
                top = jnp.max(scores[k], axis=0, keepdims=True)
                expo = jnp.exp(scores[k] - top)
                probs = expo * (1.0 / jnp.sum(expo, axis=0, keepdims=True))
                d = jnp.where(eye, probs - 1.0, probs)
                if slot + k:
                    d = jnp.where(tile < live, d, 0.0)
                ds.append(d.astype(BF))
                diffs[tile] = ds[k]
            pick_tails(jnp.minimum(pair + 1, pairs - 1), 1 - slot)
            for k in range(2):
                moves[slot, :, ats[k]] = dot_nt(qs[k], ds[k]).astype(BF)
            put_diff(pair).start()

            @pl.when(pair + 1 < pairs)
            def _():
                put_pick(pair + 1, 1 - slot).start()

    spread(pairs - 1, 1)
    for chunk, at, row, lane in places(dim, rows, hub.shape[1], grads.shape[0]):
        grads[chunk, at] = acc[row : row + 8, lane : lane + LANES].astype(BF)
    for at in range(at + 1, grads.shape[1]):
        grads[chunk, at] = jnp.zeros((8, LANES), BF)
    put_pick(pairs - 1, 1).wait()

    @pl.loop(0, pairs)
    def _(pair):
        put_diff(pair).wait()


def head_kernel(count, pick, diff, weights, heads, ent, acc, pin, din, moves, own, psem, dsem, sem):
    half = acc.shape[0] // 2
    edges = heads.shape[1]
    live = count[0, 0]
    quads = (live + 3) // 4
    pairs = 2 * quads

    def get_pick(pair):
        return pltpu.make_async_copy(pick.at[pair], pin.at[pair], psem.at[pair])

    def get_diff(pair):
        both = pl.ds(2 * pair, 2)
        return pltpu.make_async_copy(diff.at[both], din.at[both], dsem.at[pair])

    @pl.loop(0, pairs)
    def _(pair):
        get_pick(pair).start()
        get_diff(pair).start()

    get_own = pltpu.make_async_copy(ent, own, sem)
    get_own.start()
    acc[...] = jnp.zeros_like(acc)
    moves[...] = jnp.zeros_like(moves)

    def spread(pair, slot):
        acc[...] += dot_nt(moves[slot], hot(pair_ids(heads, pair), acc.shape[1]))

    @pl.loop(0, quads)
    def _(quad):
        for slot in range(2):
            pair = 2 * quad + slot
            get_pick(pair).wait()
            get_diff(pair).wait()
            ats = [slice(k * edges, (k + 1) * edges) for k in range(2)]
            d_query = [dot_nn(pin[pair, :, ats[k]], din[2 * pair + k]) for k in range(2)]
            spread(jnp.maximum(pair - 1, 0), 1 - slot)
            for k in range(2):
                w = pick_lane(weights[...], 2 * pair + k)
                dr, di = d_query[k][:half], d_query[k][half:]
                wr, wi = w[:half], w[half:]
                moves[slot, :, ats[k]] = jnp.concatenate(
                    [dr * wr + di * wi, di * wr - dr * wi], axis=0
                ).astype(BF)

    spread(pairs - 1, 1)
    get_own.wait()
    acc[...] = own[...].astype(F32) - learn_rate * acc[...]


def reorder_kernel(matching, rows, out, sems):
    puts = [
        pltpu.make_async_copy(rows.at[matching[g]], out.at[g], sems.at[g]) for g in range(out.shape[0])
    ]
    for put in puts:
        put.start()
    for put in puts:
        put.wait()


def return_kernel(matching, back, hub, out):
    own = out.shape[1] - hub.shape[1]
    total = hub[0].astype(F32)
    for m in range(1, hub.shape[0]):
        total += hub[m].astype(F32)
    total = total.astype(BF)
    for g in range(out.shape[0]):
        out[matching[g], :own] = back[g, :own]
        out[g, own:] = total


def update_kernel(base, hub, last, new_ent, new_hub):
    dim, rows = base.shape
    where = {(row, lane): (chunk, at) for chunk, at, row, lane in places(dim, rows, hub.shape[1], last.shape[0])}

    def got(row, lane):
        return jnp.concatenate([last[where[row, lane]], last[where[row + 8, lane]]], axis=0).astype(F32)

    for row in range(0, dim, 16):
        at = slice(row, row + 16)
        for lane in range(0, rows, LANES):
            to = slice(lane, lane + LANES)
            new_ent[at, to] = (base[at, to] - learn_rate * got(row, lane)).astype(BF)
        for lane in range(0, hub.shape[1], LANES):
            to = slice(lane, lane + LANES)
            new_hub[at, to] = (hub[at, to].astype(F32) - learn_rate * got(row, rows + lane)).astype(BF)


def call(kernel, out_shape, in_specs, out_specs, flops, moved, scratch=(), exps=0, vmem=32, aliases={}):
    return pl.pallas_call(
        kernel,
        out_shape=out_shape,
        in_specs=in_specs,
        out_specs=out_specs,
        scratch_shapes=scratch,
        input_output_aliases=aliases,
        compiler_params=pltpu.CompilerParams(vmem_limit_bytes=vmem * 1024 * 1024),
        cost_estimate=pl.CostEstimate(flops=flops, bytes_accessed=moved, transcendentals=exps),
    )


shape = jax.ShapeDtypeStruct


def run_weights(tile_count, tile_rel, rel):
    dim, rels = rel.shape
    rest = rels % LANES or LANES
    return call(
        weight_kernel,
        shape((dim, LANES), F32),
        [SMEM, SMEM, HBM],
        VMEM,
        40 * dim * dim * dim,
        4 * rel.size,
        [pltpu.VMEM((dim, -(-rels // LANES) * LANES), F32), pltpu.VMEM((dim, rest), F32), DMA((2,))],
        vmem=60,
    )(tile_count, tile_rel, rel)


def run_query(tile_count, ent, head_index, weights):
    dim, rows = ent.shape
    tiles, edges = head_index.shape
    return call(
        query_kernel,
        [shape((2 * tiles, dim, edges), BF), shape((2, dim, edges), BF)],
        [SMEM, VMEM, VMEM, VMEM],
        [HBM, VMEM],
        2 * tiles * edges * dim * rows,
        2 * tiles * dim * edges,
        [pltpu.VMEM((tiles // 2, 2, dim, edges), BF), DMA((tiles // 2,))],
        vmem=50,
    )(tile_count, ent, head_index, weights)


def run_tail(tile_count, query, first, partner, hub, tail_index, groups):
    tiles, edges = tail_index.shape
    dim = query.shape[1]
    rows, hubs = partner.shape[1], hub.shape[1]
    return call(
        tail_kernel,
        [
            shape((tiles, dim, 2 * edges), BF),
            shape((3 * tiles, edges, edges), BF),
            shape((groups, sum(sizes(dim, rows, hubs, groups)), 8, LANES), BF),
        ],
        [SMEM, HBM, VMEM, VMEM, VMEM, VMEM],
        [HBM, HBM, VMEM],
        4 * tiles * edges * dim * (rows + hubs + edges),
        8 * tiles * dim * edges,
        [
            pltpu.VMEM((dim, rows + hubs), BF),
            pltpu.VMEM((dim, rows + hubs), F32),
            pltpu.VMEM((tiles, dim, edges), BF),
            pltpu.VMEM((2, dim, 2 * edges), BF),
            pltpu.VMEM((tiles, edges, edges), BF),
            pltpu.VMEM((2, dim, 2 * edges), BF),
            DMA((tiles // 2,)),
            DMA((2,)),
            DMA((tiles // 2,)),
        ],
        tiles * edges * edges,
        vmem=50,
    )(tile_count, query, first, partner, hub, tail_index)


def run_head(tile_count, pick, diff, weights, head_index, ent):
    tiles, edges = head_index.shape
    dim, rows = ent.shape
    return call(
        head_kernel,
        shape((dim, rows), F32),
        [SMEM, HBM, HBM, VMEM, VMEM, HBM],
        VMEM,
        2 * tiles * edges * dim * (rows + edges),
        6 * tiles * dim * edges,
        [
            pltpu.VMEM((tiles // 2, dim, 2 * edges), BF),
            pltpu.VMEM((tiles, edges, edges), BF),
            pltpu.VMEM((2, dim, 2 * edges), BF),
            pltpu.VMEM((dim, rows), BF),
            DMA((tiles // 2,)),
            DMA((tiles // 2,)),
            DMA(()),
        ],
        vmem=50,
    )(tile_count, pick, diff, weights, head_index, ent)


def make(groups, members):
    def shards(entities, hub_rows, relations, matching, head_index, tail_index, tile_rel, tile_count):
        ent, hub, rel = entities.T, hub_rows.T, relations.T
        dim, rows = ent.shape
        hubs = hub.shape[1]
        own = sizes(dim, rows, hubs, groups)[0]

        high, wide = dim // 8, rows // LANES
        cut = ent.reshape(high, 8, wide, LANES).transpose(0, 2, 1, 3)
        cut = lax.all_to_all(cut.reshape(groups, -1, 8, LANES), "group", 0, 0)
        weights = run_weights(tile_count, tile_rel, rel)
        cut, weights = lax.optimization_barrier((cut, weights))
        cut = call(
            reorder_kernel, shape(cut.shape, BF), [SMEM, VMEM], HBM, 0, 4 * cut.size, [DMA((groups,))]
        )(matching, cut)
        partner = lax.all_to_all(cut, "group", 0, 0).reshape(high, wide, 8, LANES)
        partner = partner.transpose(0, 2, 1, 3).reshape(dim, rows)
        query, first = run_query(tile_count, ent, head_index, weights)
        pick, diff, grads = run_tail(tile_count, query, first, partner, hub, tail_index, groups)

        got = lax.all_to_all(grads, "group", 0, 0)
        got, pick, diff = lax.optimization_barrier((got, pick, diff))
        part = jnp.sum(got[:, own:].astype(F32), axis=0).astype(BF)
        other = lax.ppermute(part, "member", [(m, m ^ 1) for m in range(members)])
        part = (part.astype(F32) + other.astype(F32)).astype(BF)
        cores = [list(range(core, members, 2)) for core in range(2)]
        parts = jnp.broadcast_to(part[None], (members // 2,) + part.shape)
        parts = lax.all_to_all(parts, "member", 0, 0, axis_index_groups=cores)
        base = run_head(tile_count, pick, diff, weights, head_index, ent)
        parts, base = lax.optimization_barrier((parts, base))
        sent = call(
            return_kernel, shape(got.shape, BF), [SMEM, VMEM, VMEM], VMEM, 0, 4 * got.size
        )(matching, got, parts)
        last = lax.all_to_all(sent, "group", 0, 0)
        new_ent, new_hub = call(
            update_kernel,
            [shape((dim, rows), BF), shape((dim, hubs), BF)],
            [VMEM, VMEM, VMEM],
            [VMEM, VMEM],
            0,
            8 * dim * rows,
        )(base, hub, last)
        return (new_ent.T, new_hub.T)

    return shards


def solution(mesh):
    placed = (
        P(("group", "member"), None),
        P(),
        P(),
        P(),
        P(("group", "member"), None),
        P(("group", "member"), None),
        P(("group", "member")),
        P("group", "member"),
    )
    return jax.shard_map(
        make(mesh.shape["group"], mesh.shape["member"]),
        mesh=mesh,
        in_specs=placed,
        out_specs=(P(("group", "member"), None), P()),
        check_vma=False,
    )
```
